256 devices in a mesh: slab: 16 (over y, x), mode: 16 (over z, core).
Axes of the slice: x: 4, y: 4, z: 8, core: 2. Of those that a mesh axis runs over, the one named last changes fastest.
Arguments:
- tensor: bfloat16 [512, 131072], P('mode', 'slab'), may hold values from -24 to 24, as said below
- start_block: float32 [512, 128], replicated, may hold values from -6 to 6
Outputs:
- basis_rows: float32 [512, 128], P('mode')
- core_coeffs: float32 [131072, 128], P(('slab', 'mode'))
The draws below stay inside these ranges and needn't reach their ends.
Inputs may be any that keep to these rules, and one draw needn't show every extreme that they name: `tensor`: entries of the unfolding; each is a row factor times a column factor times a bounded random term.
All inputs are finite; a program needn't handle non-finite values.
Results may differ from the reference program's by a relative error of at most 0.0029.
Values may be sent and summed in bfloat16 or wider, within the bound.
A program may use at most 64 MiB of HBM per device.

```python
import jax
import jax.numpy as jnp
from jax import lax

M = 512
R = 128
COLS = 131072


def draw_tensor(key, part):
    keys = jax.random.split(jax.random.fold_in(key, 7), 3)
    row_scale = jnp.exp(jax.random.uniform(keys[0], (M, 1), jnp.float32) * jnp.log(2.0))
    ramp = jnp.exp(jnp.log(3.0) * jnp.arange(COLS, dtype=jnp.float32) / COLS)
    col_scale = 0.3 * ramp * jnp.exp(jax.random.uniform(keys[1], (COLS,), jnp.float32) * jnp.log(10.0 / 3.0))
    noise = jax.random.truncated_normal(keys[2], -4.0, 4.0, (M, COLS), jnp.float32)
    return (row_scale * col_scale[None, :] * noise).astype(jnp.bfloat16)


def gaussian(own_key, shape, width, bound, kind=jnp.bfloat16):
    return jnp.clip(width * jax.random.normal(own_key, shape, jnp.float32), -bound, bound).astype(kind)


def setup_inputs(seed: int = 0) -> dict:
    key_list = jax.random.split(jax.random.key(seed), 3)
    tensor = draw_tensor(jax.random.fold_in(key_list[2], 71), 0)
    start_block = gaussian(key_list[1], (M, R), 1.0, 6.0, jnp.float32)
    return {"tensor": tensor, "start_block": start_block}


highest = lax.Precision.HIGHEST
contract_cols = (((1,), (1,)), ((), ()))
contract_rows = (((0,), (0,)), ((), ()))

def orthonormal(image_block):
    small_gram = jnp.dot(image_block.T, image_block, precision=highest)
    factor = jnp.linalg.cholesky(small_gram)
    return lax.linalg.triangular_solve(factor, image_block, left_side=False, lower=True, transpose_a=True)

def reference(tensor, start_block):
    gram_total = lax.dot_general(tensor.astype(jnp.float32), tensor.astype(jnp.float32), contract_cols, preferred_element_type=jnp.float32)
    image_block = jnp.dot(gram_total, start_block, precision=highest)
    basis_rows = orthonormal(image_block)
    basis_low = basis_rows.astype(jnp.bfloat16)
    core_coeffs = lax.dot_general(tensor.astype(jnp.float32), basis_low.astype(jnp.float32), contract_rows, preferred_element_type=jnp.float32)
    return (basis_rows, core_coeffs)
```

```python
import functools

import jax
import jax.numpy as jnp
from jax import lax
from jax.experimental import pallas as pl
from jax.experimental.pallas import tpu as pltpu
from jax.sharding import PartitionSpec as P

MESH = pl.DeviceIdType.MESH
highest = lax.Precision.HIGHEST
BF16, F32 = jnp.bfloat16, jnp.float32


def exchange(sizes, tensor_ref, start_ref, regrouped_out, image_ref,
             regrouped, split_start, partial_low, plane_in, z_in, mine,
             own_sem, out_sem, a2a_send, a2a_recv, rs_send, rs_recv,
             z_send, z_recv, ag_send, ag_recv):
    slabs, modes = sizes
    chips_z, plane = modes // 2, slabs * 2
    rows, block = tensor_ref.shape[0], regrouped.shape[1]
    piece = plane_in.shape[1]
    slab, mode = lax.axis_index("slab"), lax.axis_index("mode")
    z, core = mode // 2, lax.rem(mode, 2)
    spot = slab * 2 + core

    def z_peer(dz, flip):
        peer_core = core if flip == 0 else 1 - core
        return lax.rem(z + dz + chips_z, chips_z) * 2 + peer_core

    def plane_peer(ds, flip):
        peer_core = core if flip == 0 else 1 - core
        return lax.rem(slab + ds + slabs, slabs), peer_core

    half = chips_z // 2
    order = [half]
    for distance in range(half - 1, 0, -1):
        order += [distance, -distance]
    z_steps = [(dz, flip) for dz in order for flip in (0, 1)] + [(0, 1)]
    plane_steps = [(ds, flip) for ds in range(1, slabs) for flip in (0, 1)] + [(0, 1)]

    barrier = pltpu.get_barrier_semaphore()
    for dz, flip in z_steps:
        pl.semaphore_signal(barrier, inc=1, device_id=(slab, z_peer(dz, flip)), device_id_type=MESH)
    for ds, flip in plane_steps[:-1]:
        other, peer_core = plane_peer(ds, flip)
        pl.semaphore_signal(barrier, inc=1, device_id=(other, z * 2 + peer_core), device_id_type=MESH)
    own = pltpu.make_async_copy(
        tensor_ref.at[:, pl.ds(pl.multiple_of(mode * block, block), block)],
        regrouped.at[pl.ds(pl.multiple_of(mode * rows, rows), rows), :],
        own_sem,
    )
    own.start()
    pl.semaphore_wait(barrier, len(z_steps) + len(plane_steps) - 1)

    def a2a(index, dz, flip, landing):
        peer = z_peer(dz, flip)
        return pltpu.make_async_remote_copy(
            src_ref=tensor_ref.at[:, pl.ds(pl.multiple_of(peer * block, block), block)],
            dst_ref=regrouped.at[pl.ds(pl.multiple_of(landing * rows, rows), rows), :],
            send_sem=a2a_send.at[index],
            recv_sem=a2a_recv.at[index],
            device_id=(slab, peer),
            device_id_type=MESH,
        )

    for index, (dz, flip) in enumerate(z_steps):
        a2a(index, dz, flip, mode).start()

    start_t = start_ref[...].T
    high = start_t.astype(BF16)
    split_start[0] = high
    split_start[1] = (start_t - high.astype(F32)).astype(BF16)

    own.wait()
    for index, (dz, flip) in enumerate(z_steps):
        a2a(index, dz, flip, z_peer(-dz, flip)).wait_recv()

    out = pltpu.make_async_copy(regrouped, regrouped_out, out_sem)
    out.start()
    whole = regrouped[...]
    projected = jnp.dot(split_start[0], whole, preferred_element_type=F32)
    projected += jnp.dot(split_start[1], whole, preferred_element_type=F32)
    high = projected.astype(BF16)
    low = (projected - high.astype(F32)).astype(BF16)
    last = (((1,), (1,)), ((), ()))
    partial = lax.dot_general(whole, high, last, preferred_element_type=F32)
    partial += lax.dot_general(whole, low, last, preferred_element_type=F32)
    partial_low[...] = partial.astype(BF16).reshape(partial_low.shape)

    def scatter(index, ds, flip, landing):
        other, peer_core = plane_peer(ds, flip)
        return pltpu.make_async_remote_copy(
            src_ref=partial_low.at[other * 2 + peer_core],
            dst_ref=plane_in.at[landing],
            send_sem=rs_send.at[index],
            recv_sem=rs_recv.at[index],
            device_id=(other, z * 2 + peer_core),
            device_id_type=MESH,
        )

    for index, (ds, flip) in enumerate(plane_steps):
        scatter(index, ds, flip, spot).start()
    plane_in[spot] = partial_low[spot]
    for index, (ds, flip) in enumerate(plane_steps):
        other, peer_core = plane_peer(-ds, flip)
        scatter(index, ds, flip, other * 2 + peer_core).wait_recv()
    mine[...] = jnp.sum(plane_in[...].astype(F32), axis=0)
    z_in[z] = mine[...]

    def along_z(index, dz, landing):
        peer = z_peer(dz, 0)
        return pltpu.make_async_remote_copy(
            src_ref=mine,
            dst_ref=z_in.at[landing],
            send_sem=z_send.at[index],
            recv_sem=z_recv.at[index],
            device_id=(slab, peer),
            device_id_type=MESH,
        )

    for index, dz in enumerate(order):
        along_z(index, dz, z).start()
    for index, dz in enumerate(order):
        along_z(index, dz, lax.rem(z - dz + chips_z, chips_z)).wait_recv()
    image_ref[spot] = jnp.sum(z_in[...], axis=0)

    def gather(index, ds, flip, landing):
        other, peer_core = plane_peer(ds, flip)
        return pltpu.make_async_remote_copy(
            src_ref=image_ref.at[spot],
            dst_ref=image_ref.at[landing],
            send_sem=ag_send.at[index],
            recv_sem=ag_recv.at[index],
            device_id=(other, z * 2 + peer_core),
            device_id_type=MESH,
        )

    for index, (ds, flip) in enumerate(plane_steps):
        gather(index, ds, flip, spot).start()
    for index, (ds, flip) in enumerate(plane_steps):
        other, peer_core = plane_peer(-ds, flip)
        gather(index, ds, flip, other * 2 + peer_core).wait_recv()

    for index, (dz, flip) in enumerate(z_steps):
        a2a(index, dz, flip, mode).wait_send()
    for index, (ds, flip) in enumerate(plane_steps):
        scatter(index, ds, flip, spot).wait_send()
        gather(index, ds, flip, spot).wait_send()
    for index, dz in enumerate(order):
        along_z(index, dz, z).wait_send()
    out.wait()


def orthonormal(image_block):
    small_gram = jnp.dot(image_block.T, image_block, precision=highest)
    factor = jnp.linalg.cholesky(small_gram)
    return lax.linalg.triangular_solve(
        factor, image_block, left_side=False, lower=True, transpose_a=True
    )


def shards(sizes, tensor, start_block):
    slabs, modes = sizes
    rows, width = tensor.shape
    full, rank = start_block.shape
    block = width // modes
    plane = slabs * 2
    piece = full // plane
    dma = pltpu.SemaphoreType.DMA
    regrouped, image = pl.pallas_call(
        functools.partial(exchange, sizes),
        out_shape=(
            jax.ShapeDtypeStruct((full, block), BF16),
            jax.ShapeDtypeStruct((plane, piece, rank), F32),
        ),
        in_specs=[pl.BlockSpec(memory_space=pl.ANY), pl.BlockSpec(memory_space=pltpu.VMEM)],
        out_specs=(pl.BlockSpec(memory_space=pl.ANY), pl.BlockSpec(memory_space=pltpu.VMEM)),
        scratch_shapes=[
            pltpu.VMEM((full, block), BF16),
            pltpu.VMEM((2, rank, full), BF16),
            pltpu.VMEM((plane, piece, rank), BF16),
            pltpu.VMEM((plane, piece, rank), BF16),
            pltpu.VMEM((modes // 2, piece, rank), F32),
            pltpu.VMEM((piece, rank), F32),
            dma, dma,
            dma((modes,)), dma((modes,)),
            dma((plane,)), dma((plane,)),
            dma((modes // 2,)), dma((modes // 2,)),
            dma((plane,)), dma((plane,)),
        ],
        compiler_params=pltpu.CompilerParams(collective_id=0, has_side_effects=True),
        name="exchange",
    )(tensor, start_block)
    basis_full = orthonormal(image.reshape(full, rank))
    basis_low = basis_full.astype(BF16)
    basis_rows = lax.dynamic_slice_in_dim(basis_full, lax.axis_index("mode") * rows, rows, 0)
    core_coeffs = lax.dot_general(
        regrouped, basis_low, (((0,), (0,)), ((), ())), preferred_element_type=F32
    )
    return (basis_rows, core_coeffs)


def solution(mesh):
    sizes = (mesh.shape["slab"], mesh.shape["mode"])
    return jax.shard_map(
        functools.partial(shards, sizes),
        mesh=mesh,
        in_specs=(P("mode", "slab"), P()),
        out_specs=(P("mode", None), P(("slab", "mode"), None)),
        check_vma=False,
    )
```

```python
import functools

import jax
import jax.numpy as jnp
from jax import lax
from jax.experimental import pallas as pl
from jax.experimental.pallas import tpu as pltpu
from jax.sharding import PartitionSpec as P

MESH = pl.DeviceIdType.MESH
highest = lax.Precision.HIGHEST
BF16, F32 = jnp.bfloat16, jnp.float32


def exchange(sizes, tensor_ref, start_ref, regrouped_out, image_ref,
             regrouped, split_start, partial_low, plane_in, z_in, mine,
             own_sem, out_sem, a2a_send, a2a_recv, rs_send, rs_recv,
             z_send, z_recv, ag_send, ag_recv):
    slabs, modes = sizes
    chips_z, plane = modes // 2, slabs * 2
    rows, block = tensor_ref.shape[0], regrouped.shape[1]
    piece = plane_in.shape[1]
    slab, mode = lax.axis_index("slab"), lax.axis_index("mode")
    z, core = mode // 2, lax.rem(mode, 2)
    spot = slab * 2 + core

    def z_peer(dz, flip):
        peer_core = core if flip == 0 else 1 - core
        return lax.rem(z + dz + chips_z, chips_z) * 2 + peer_core

    def plane_peer(ds, flip):
        peer_core = core if flip == 0 else 1 - core
        return lax.rem(slab + ds + slabs, slabs), peer_core

    half = chips_z // 2
    order = [half]
    for distance in range(half - 1, 0, -1):
        order += [distance, -distance]
    z_steps = [(dz, flip) for dz in order for flip in (0, 1)] + [(0, 1)]
    plane_steps = [(ds, flip) for ds in range(1, slabs) for flip in (0, 1)] + [(0, 1)]

    barrier = pltpu.get_barrier_semaphore()
    for dz, flip in z_steps:
        pl.semaphore_signal(barrier, inc=1, device_id=(slab, z_peer(dz, flip)), device_id_type=MESH)
    for ds, flip in plane_steps[:-1]:
        other, peer_core = plane_peer(ds, flip)
        pl.semaphore_signal(barrier, inc=1, device_id=(other, z * 2 + peer_core), device_id_type=MESH)
    own = pltpu.make_async_copy(
        tensor_ref.at[:, pl.ds(pl.multiple_of(mode * block, block), block)],
        regrouped.at[pl.ds(pl.multiple_of(mode * rows, rows), rows), :],
        own_sem,
    )
    own.start()
    pl.semaphore_wait(barrier, len(z_steps) + len(plane_steps) - 1)

    def a2a(index, dz, flip, landing):
        peer = z_peer(dz, flip)
        return pltpu.make_async_remote_copy(
            src_ref=tensor_ref.at[:, pl.ds(pl.multiple_of(peer * block, block), block)],
            dst_ref=regrouped.at[pl.ds(pl.multiple_of(landing * rows, rows), rows), :],
            send_sem=a2a_send.at[index],
            recv_sem=a2a_recv.at[index],
            device_id=(slab, peer),
            device_id_type=MESH,
        )

    for index, (dz, flip) in enumerate(z_steps):
        a2a(index, dz, flip, mode).start()

    start_t = start_ref[...].T
    high = start_t.astype(BF16)
    split_start[0] = high
    split_start[1] = (start_t - high.astype(F32)).astype(BF16)

    own.wait()
    for index, (dz, flip) in enumerate(z_steps):
        a2a(index, dz, flip, z_peer(-dz, flip)).wait_recv()

    out = pltpu.make_async_copy(regrouped, regrouped_out, out_sem)
    out.start()
    whole = regrouped[...]
    projected = jnp.dot(split_start[0], whole, preferred_element_type=F32)
    projected += jnp.dot(split_start[1], whole, preferred_element_type=F32)
    high = projected.astype(BF16)
    low = (projected - high.astype(F32)).astype(BF16)
    last = (((1,), (1,)), ((), ()))
    partial = lax.dot_general(whole, high, last, preferred_element_type=F32)
    partial += lax.dot_general(whole, low, last, preferred_element_type=F32)
    partial_low[...] = partial.astype(BF16).reshape(partial_low.shape)

    def scatter(index, ds, flip, landing):
        other, peer_core = plane_peer(ds, flip)
        return pltpu.make_async_remote_copy(
            src_ref=partial_low.at[other * 2 + peer_core],
            dst_ref=plane_in.at[landing],
            send_sem=rs_send.at[index],
            recv_sem=rs_recv.at[index],
            device_id=(other, z * 2 + peer_core),
            device_id_type=MESH,
        )

    for index, (ds, flip) in enumerate(plane_steps):
        scatter(index, ds, flip, spot).start()
    plane_in[spot] = partial_low[spot]
    for index, (ds, flip) in enumerate(plane_steps):
        other, peer_core = plane_peer(-ds, flip)
        scatter(index, ds, flip, other * 2 + peer_core).wait_recv()
    mine[...] = jnp.sum(plane_in[...].astype(F32), axis=0)
    z_in[z] = mine[...]

    def along_z(index, dz, landing):
        peer = z_peer(dz, 0)
        return pltpu.make_async_remote_copy(
            src_ref=mine,
            dst_ref=z_in.at[landing],
            send_sem=z_send.at[index],
            recv_sem=z_recv.at[index],
            device_id=(slab, peer),
            device_id_type=MESH,
        )

    for index, dz in enumerate(order):
        along_z(index, dz, z).start()
    for index, dz in enumerate(order):
        along_z(index, dz, lax.rem(z - dz + chips_z, chips_z)).wait_recv()
    image_ref[spot] = jnp.sum(z_in[...], axis=0)

    def gather(index, ds, flip, landing):
        other, peer_core = plane_peer(ds, flip)
        return pltpu.make_async_remote_copy(
            src_ref=image_ref.at[spot],
            dst_ref=image_ref.at[landing],
            send_sem=ag_send.at[index],
            recv_sem=ag_recv.at[index],
            device_id=(other, z * 2 + peer_core),
            device_id_type=MESH,
        )

    for index, (ds, flip) in enumerate(plane_steps):
        gather(index, ds, flip, spot).start()
    for index, (ds, flip) in enumerate(plane_steps):
        other, peer_core = plane_peer(-ds, flip)
        gather(index, ds, flip, other * 2 + peer_core).wait_recv()

    for index, (dz, flip) in enumerate(z_steps):
        a2a(index, dz, flip, mode).wait_send()
    for index, (ds, flip) in enumerate(plane_steps):
        scatter(index, ds, flip, spot).wait_send()
        gather(index, ds, flip, spot).wait_send()
    for index, dz in enumerate(order):
        along_z(index, dz, z).wait_send()
    out.wait()


def inverse_factor(gram):
    n = gram.shape[0]
    tall = n // 8
    lane = lax.broadcasted_iota(jnp.int32, (8, n), 1)
    sub = lax.broadcasted_iota(jnp.int32, (8, n), 0)
    spread = lambda x, k: jnp.broadcast_to(x[:, k : k + 1], (8, n))
    pick = lambda x, k: jnp.broadcast_to(x[k : k + 1], (8, n))
    work = [gram[8 * r : 8 * r + 8, :] for r in range(tall)]
    out = []
    ahead = [spread(work[0], k) for k in range(8)]
    for p in range(tall):
        below = range(p, tall)
        cols = [{r: ahead[k] if r == p else spread(work[r], 8 * p + k) for r in below} for k in range(8)]
        if p + 1 < tall:
            ahead = [spread(work[p + 1], 8 * (p + 1) + k) for k in range(8)]
        done = jnp.zeros((8, n), F32)
        for s in range(0, 8, 2):
            j = 8 * p + s
            col_a, col_b = cols[s], cols[s + 1]
            a, b, c = pick(col_a[p], s), pick(col_a[p], s + 1), pick(col_b[p], s + 1)
            det = a * c - b * b
            inv = 1.0 / det
            ia, ib, ic = c * inv, b * inv, a * inv
            for k in range(s + 2, 8):
                va, vb = pick(col_a[p], k), pick(col_b[p], k)
                ta, tb = ia * va - ib * vb, ic * vb - ib * va
                for r in below:
                    cols[k][r] = cols[k][r] - (col_a[r] * ta + col_b[r] * tb)
            if p + 1 < tall:
                for k in range(8):
                    va, vb = pick(col_a[p + 1], k), pick(col_b[p + 1], k)
                    ta, tb = ia * va - ib * vb, ic * vb - ib * va
                    ahead[k] = ahead[k] - (col_a[p + 1] * ta + col_b[p + 1] * tb)
            row_a, row_b = pick(work[p], s), pick(work[p], s + 1)
            unit_a = jnp.where(lane == j, 1.0, 0.0).astype(F32)
            unit_b = jnp.where(lane == j + 1, 1.0, 0.0).astype(F32)
            full_a, full_b = row_a + unit_a, row_b + unit_b
            ta = ia * full_a - ib * full_b
            tb = ic * full_b - ib * full_a
            left_a = jnp.where(lane < j, row_a, unit_a)
            left_b = jnp.where(lane < j, row_b, unit_b)
            root_a = lax.rsqrt(a)
            root_b = lax.rsqrt(det * (root_a * root_a))
            w_a = left_a * root_a
            w_b = (left_b - (b * root_a) * w_a) * root_b
            done = jnp.where(sub == s, w_a, jnp.where(sub == s + 1, w_b, done))
            for r in below:
                work[r] = work[r] - (col_a[r] * ta + col_b[r] * tb)
        out.append(done)
    return jnp.concatenate(out, axis=0)


def finish(regrouped_ref, image_ref, rows_ref, core_ref, basis):
    image = image_ref[...].reshape(basis.shape)
    image = image * lax.rsqrt(jnp.sum(image * image, axis=0, keepdims=True))
    across = (((0,), (0,)), ((), ()))
    gram = lax.dot_general(image, image, across, precision=highest, preferred_element_type=F32)
    inverse = inverse_factor(gram)
    whole = lax.dot_general(
        image, inverse, (((1,), (1,)), ((), ())), precision=highest, preferred_element_type=F32
    )
    basis[...] = whole
    count = rows_ref.shape[0]
    rows_ref[...] = basis[pl.ds(pl.multiple_of(lax.axis_index("mode") * count, count), count), :]
    core_ref[...] = lax.dot_general(
        regrouped_ref[...], whole.astype(BF16), across, preferred_element_type=F32
    )


def shards(sizes, tensor, start_block):
    slabs, modes = sizes
    rows, width = tensor.shape
    full, rank = start_block.shape
    block = width // modes
    plane = slabs * 2
    piece = full // plane
    dma = pltpu.SemaphoreType.DMA
    regrouped, image = pl.pallas_call(
        functools.partial(exchange, sizes),
        out_shape=(
            jax.ShapeDtypeStruct((full, block), BF16),
            jax.ShapeDtypeStruct((plane, piece, rank), F32),
        ),
        in_specs=[pl.BlockSpec(memory_space=pl.ANY), pl.BlockSpec(memory_space=pltpu.VMEM)],
        out_specs=(pl.BlockSpec(memory_space=pl.ANY), pl.BlockSpec(memory_space=pltpu.VMEM)),
        scratch_shapes=[
            pltpu.VMEM((full, block), BF16),
            pltpu.VMEM((2, rank, full), BF16),
            pltpu.VMEM((plane, piece, rank), BF16),
            pltpu.VMEM((plane, piece, rank), BF16),
            pltpu.VMEM((modes // 2, piece, rank), F32),
            pltpu.VMEM((piece, rank), F32),
            dma, dma,
            dma((modes,)), dma((modes,)),
            dma((plane,)), dma((plane,)),
            dma((modes // 2,)), dma((modes // 2,)),
            dma((plane,)), dma((plane,)),
        ],
        compiler_params=pltpu.CompilerParams(collective_id=0, has_side_effects=True),
        name="exchange",
    )(tensor, start_block)
    return pl.pallas_call(
        finish,
        out_shape=(
            jax.ShapeDtypeStruct((rows, rank), F32),
            jax.ShapeDtypeStruct((block, rank), F32),
        ),
        scratch_shapes=[pltpu.VMEM((full, rank), F32)],
        name="finish",
    )(regrouped, image)


def solution(mesh):
    sizes = (mesh.shape["slab"], mesh.shape["mode"])
    return jax.shard_map(
        functools.partial(shards, sizes),
        mesh=mesh,
        in_specs=(P("mode", "slab"), P()),
        out_specs=(P("mode", None), P(("slab", "mode"), None)),
        check_vma=False,
    )
```

```python
import functools

import jax
import jax.numpy as jnp
from jax import lax
from jax.experimental import pallas as pl
from jax.experimental.pallas import tpu as pltpu
from jax.sharding import PartitionSpec as P

MESH = pl.DeviceIdType.MESH
highest = lax.Precision.HIGHEST
BF16, F32 = jnp.bfloat16, jnp.float32


def exchange(sizes, tensor_ref, start_ref, turned_ref, image_ref,
             regrouped, split_start, partial_low, plane_in, z_in, mine,
             own_sem, z_known, x_known, core_known, y_known, a2a_send, a2a_recv, rs_send, rs_recv,
             z_send, z_recv, ag_send, ag_recv):
    slabs, modes = sizes
    chips_z, plane = modes // 2, slabs * 2
    rows, block = tensor_ref.shape[0], regrouped.shape[1]
    piece = plane_in.shape[1]
    slab, mode = lax.axis_index("slab"), lax.axis_index("mode")
    z, core = mode // 2, lax.rem(mode, 2)
    spot = slab * 2 + core

    def z_peer(dz, flip):
        peer_core = core if flip == 0 else 1 - core
        return lax.rem(z + dz + chips_z, chips_z) * 2 + peer_core

    def plane_peer(ds, flip):
        peer_core = core if flip == 0 else 1 - core
        return lax.rem(slab + ds + slabs, slabs), peer_core

    half = chips_z // 2
    order = [half]
    for distance in range(half - 1, 0, -1):
        order += [distance, -distance]
    z_steps = [(dz, flip) for dz in order for flip in (0, 1)] + [(0, 1)]
    plane_steps = [(ds, flip) for ds in range(1, slabs) for flip in (0, 1)] + [(0, 1)]

    side = 4
    x, y = lax.rem(slab, side), slab // side
    x_beside = [(y * side + lax.rem(x + d, side), mode) for d in (1, side - 1)]
    y_beside = [(lax.rem(y + d, side) * side + x, mode) for d in (1, side - 1)]
    z_beside = [(slab, z_peer(dz, 0)) for dz in (1, -1)]
    other_core = (slab, z_peer(0, 1))

    def tell(semaphore, device):
        pl.semaphore_signal(semaphore, inc=1, device_id=device, device_id_type=MESH)

    barrier = pltpu.get_barrier_semaphore()
    beside = z_beside + [(slab, z_peer(dz, 1)) for dz in (1, -1)] + [other_core] + x_beside + y_beside
    for device in beside:
        tell(barrier, device)
    own = pltpu.make_async_copy(
        tensor_ref.at[:, pl.ds(pl.multiple_of(mode * block, block), block)],
        regrouped.at[pl.ds(pl.multiple_of(mode * rows, rows), rows), :],
        own_sem,
    )
    own.start()
    start_t = start_ref[...].T
    high = start_t.astype(BF16)
    split_start[0] = high
    split_start[1] = (start_t - high.astype(F32)).astype(BF16)
    pl.semaphore_wait(barrier, len(beside))

    def a2a(index, dz, flip, landing):
        peer = z_peer(dz, flip)
        return pltpu.make_async_remote_copy(
            src_ref=tensor_ref.at[:, pl.ds(pl.multiple_of(peer * block, block), block)],
            dst_ref=regrouped.at[pl.ds(pl.multiple_of(landing * rows, rows), rows), :],
            send_sem=a2a_send.at[index],
            recv_sem=a2a_recv.at[index],
            device_id=(slab, peer),
            device_id_type=MESH,
        )

    def send(distances):
        for index, (dz, flip) in enumerate(z_steps):
            if dz in distances:
                a2a(index, dz, flip, mode).start()

    def reach(known, devices):
        for way in (0, 1):
            tell(known.at[way], devices[way])

    def heard(known):
        for way in (0, 1):
            pl.semaphore_wait(known.at[way], 1)

    reach(z_known.at[0], z_beside)
    reach(x_known, x_beside)
    send((1, -1, 0))
    for further in range(1, half):
        heard(z_known.at[further - 1])
        if further + 1 < half:
            reach(z_known.at[further], z_beside)
        if further == 1:
            send((2, -2))
    send([dz for dz in order if abs(dz) > 2])
    heard(x_known)
    tell(core_known, other_core)
    pl.semaphore_wait(core_known, 1)
    reach(y_known.at[0], y_beside)
    heard(y_known.at[0])
    reach(y_known.at[1], y_beside)
    heard(y_known.at[1])

    own.wait()
    for index, (dz, flip) in enumerate(z_steps):
        a2a(index, dz, flip, z_peer(-dz, flip)).wait_recv()

    whole = regrouped[...]
    projected = jnp.dot(split_start[0], whole, preferred_element_type=F32)
    projected += jnp.dot(split_start[1], whole, preferred_element_type=F32)
    high = projected.astype(BF16)
    low = (projected - high.astype(F32)).astype(BF16)
    last = (((1,), (1,)), ((), ()))
    partial = lax.dot_general(whole, high, last, preferred_element_type=F32)
    partial += lax.dot_general(whole, low, last, preferred_element_type=F32)
    partial_low[...] = partial.astype(BF16).reshape(partial_low.shape)

    def scatter(index, ds, flip, landing):
        other, peer_core = plane_peer(ds, flip)
        return pltpu.make_async_remote_copy(
            src_ref=partial_low.at[other * 2 + peer_core],
            dst_ref=plane_in.at[landing],
            send_sem=rs_send.at[index],
            recv_sem=rs_recv.at[index],
            device_id=(other, z * 2 + peer_core),
            device_id_type=MESH,
        )

    for index, (ds, flip) in enumerate(plane_steps):
        scatter(index, ds, flip, spot).start()
    plane_in[spot] = partial_low[spot]
    turned_ref[...] = regrouped[...].T
    for index, (ds, flip) in enumerate(plane_steps):
        other, peer_core = plane_peer(-ds, flip)
        scatter(index, ds, flip, other * 2 + peer_core).wait_recv()
    mine[...] = jnp.sum(plane_in[...].astype(F32), axis=0)
    z_in[z] = mine[...]

    def along_z(index, dz, landing):
        peer = z_peer(dz, 0)
        return pltpu.make_async_remote_copy(
            src_ref=mine,
            dst_ref=z_in.at[landing],
            send_sem=z_send.at[index],
            recv_sem=z_recv.at[index],
            device_id=(slab, peer),
            device_id_type=MESH,
        )

    for index, dz in enumerate(order):
        along_z(index, dz, z).start()
    for index, dz in enumerate(order):
        along_z(index, dz, lax.rem(z - dz + chips_z, chips_z)).wait_recv()
    image_ref[spot] = jnp.sum(z_in[...], axis=0)

    def gather(index, ds, flip, landing):
        other, peer_core = plane_peer(ds, flip)
        return pltpu.make_async_remote_copy(
            src_ref=image_ref.at[spot],
            dst_ref=image_ref.at[landing],
            send_sem=ag_send.at[index],
            recv_sem=ag_recv.at[index],
            device_id=(other, z * 2 + peer_core),
            device_id_type=MESH,
        )

    for index, (ds, flip) in enumerate(plane_steps):
        gather(index, ds, flip, spot).start()
    for index, (ds, flip) in enumerate(plane_steps):
        other, peer_core = plane_peer(-ds, flip)
        gather(index, ds, flip, other * 2 + peer_core).wait_recv()

    for index, (dz, flip) in enumerate(z_steps):
        a2a(index, dz, flip, mode).wait_send()
    for index, (ds, flip) in enumerate(plane_steps):
        scatter(index, ds, flip, spot).wait_send()
        gather(index, ds, flip, spot).wait_send()
    for index, dz in enumerate(order):
        along_z(index, dz, z).wait_send()


def inverse_factor(gram):
    n = gram.shape[0]
    tall = n // 8
    lane = lax.broadcasted_iota(jnp.int32, (8, n), 1)
    sub = lax.broadcasted_iota(jnp.int32, (8, n), 0)
    spread = lambda x, k: jnp.broadcast_to(x[:, k : k + 1], (8, n))
    pick = lambda x, k: jnp.broadcast_to(x[k : k + 1], (8, n))
    work = [gram[8 * r : 8 * r + 8, :] for r in range(tall)]
    out = []
    ahead = [spread(work[0], k) for k in range(8)]
    for p in range(tall):
        below = range(p, tall)
        cols = [{r: ahead[k] if r == p else spread(work[r], 8 * p + k) for r in below} for k in range(8)]
        if p + 1 < tall:
            ahead = [spread(work[p + 1], 8 * (p + 1) + k) for k in range(8)]
        done = jnp.zeros((8, n), F32)
        for s in range(0, 8, 2):
            j = 8 * p + s
            col_a, col_b = cols[s], cols[s + 1]
            a, b, c = pick(col_a[p], s), pick(col_a[p], s + 1), pick(col_b[p], s + 1)
            det = a * c - b * b
            inv = 1.0 / det
            ia, ib, ic = c * inv, b * inv, a * inv
            for k in range(s + 2, 8):
                va, vb = pick(col_a[p], k), pick(col_b[p], k)
                ta, tb = ia * va - ib * vb, ic * vb - ib * va
                for r in below:
                    cols[k][r] = cols[k][r] - (col_a[r] * ta + col_b[r] * tb)
            if p + 1 < tall:
                for k in range(8):
                    va, vb = pick(col_a[p + 1], k), pick(col_b[p + 1], k)
                    ta, tb = ia * va - ib * vb, ic * vb - ib * va
                    ahead[k] = ahead[k] - (col_a[p + 1] * ta + col_b[p + 1] * tb)
            row_a, row_b = pick(work[p], s), pick(work[p], s + 1)
            unit_a = jnp.where(lane == j, 1.0, 0.0).astype(F32)
            unit_b = jnp.where(lane == j + 1, 1.0, 0.0).astype(F32)
            full_a, full_b = row_a + unit_a, row_b + unit_b
            ta = ia * full_a - ib * full_b
            tb = ic * full_b - ib * full_a
            left_a = jnp.where(lane < j, row_a, unit_a)
            left_b = jnp.where(lane < j, row_b, unit_b)
            root_a = lax.rsqrt(a)
            root_b = lax.rsqrt(det * (root_a * root_a))
            w_a = left_a * root_a
            w_b = (left_b - (b * root_a) * w_a) * root_b
            done = jnp.where(sub == s, w_a, jnp.where(sub == s + 1, w_b, done))
            for r in below:
                work[r] = work[r] - (col_a[r] * ta + col_b[r] * tb)
        out.append(done)
    return jnp.concatenate(out, axis=0)


def finish(turned_ref, image_ref, rows_ref, core_ref, basis):
    image = image_ref[...].reshape(basis.shape)
    image = image * lax.rsqrt(jnp.sum(image * image, axis=0, keepdims=True))
    across = (((0,), (0,)), ((), ()))
    gram = lax.dot_general(image, image, across, precision=highest, preferred_element_type=F32)
    inverse = inverse_factor(gram)
    whole = lax.dot_general(
        image, inverse, (((1,), (1,)), ((), ())), precision=highest, preferred_element_type=F32
    )
    basis[...] = whole
    count = rows_ref.shape[0]
    rows_ref[...] = basis[pl.ds(pl.multiple_of(lax.axis_index("mode") * count, count), count), :]
    core_ref[...] = jnp.dot(turned_ref[...], whole.astype(BF16), preferred_element_type=F32)


def shards(sizes, tensor, start_block):
    slabs, modes = sizes
    rows, width = tensor.shape
    full, rank = start_block.shape
    block = width // modes
    plane = slabs * 2
    piece = full // plane
    dma, regular = pltpu.SemaphoreType.DMA, pltpu.SemaphoreType.REGULAR
    turned, image = pl.pallas_call(
        functools.partial(exchange, sizes),
        out_shape=(
            pltpu.VMEM((block, full), BF16),
            pltpu.VMEM((plane, piece, rank), F32),
        ),
        in_specs=[pl.BlockSpec(memory_space=pl.ANY), pl.BlockSpec(memory_space=pltpu.VMEM)],
        out_specs=(pl.BlockSpec(memory_space=pltpu.VMEM), pl.BlockSpec(memory_space=pltpu.VMEM)),
        scratch_shapes=[
            pltpu.VMEM((full, block), BF16),
            pltpu.VMEM((2, rank, full), BF16),
            pltpu.VMEM((plane, piece, rank), BF16),
            pltpu.VMEM((plane, piece, rank), BF16),
            pltpu.VMEM((modes // 2, piece, rank), F32),
            pltpu.VMEM((piece, rank), F32),
            dma,
            regular((modes // 4 - 1, 2)), regular((2,)), regular, regular((2, 2)),
            dma((modes,)), dma((modes,)),
            dma((plane,)), dma((plane,)),
            dma((modes // 2,)), dma((modes // 2,)),
            dma((plane,)), dma((plane,)),
        ],
        compiler_params=pltpu.CompilerParams(collective_id=0, has_side_effects=True),
        name="exchange",
    )(tensor, start_block)
    return pl.pallas_call(
        finish,
        out_shape=(
            jax.ShapeDtypeStruct((rows, rank), F32),
            jax.ShapeDtypeStruct((block, rank), F32),
        ),
        in_specs=[pl.BlockSpec(memory_space=pltpu.VMEM)] * 2,
        scratch_shapes=[pltpu.VMEM((full, rank), F32)],
        name="finish",
    )(*(pltpu.with_memory_space_constraint(x, pltpu.VMEM) for x in (turned, image)))


def solution(mesh):
    sizes = (mesh.shape["slab"], mesh.shape["mode"])
    return jax.shard_map(
        functools.partial(shards, sizes),
        mesh=mesh,
        in_specs=(P("mode", "slab"), P()),
        out_specs=(P("mode", None), P(("slab", "mode"), None)),
        check_vma=False,
    )
```

```python
import functools

import jax
import jax.numpy as jnp
from jax import lax
from jax.experimental import pallas as pl
from jax.experimental.pallas import tpu as pltpu
from jax.sharding import PartitionSpec as P

MESH = pl.DeviceIdType.MESH
highest = lax.Precision.HIGHEST
BF16, F32 = jnp.bfloat16, jnp.float32


def exchange(sizes, tensor_ref, start_ref, turned_ref, image_ref,
             start, regrouped, split_start, partial_low, plane_in, z_in, mine,
             start_sem, own_sem, z_known, x_known, core_known, y_known, a2a_send, a2a_recv, rs_send, rs_recv,
             z_send, z_recv, ag_send, ag_recv):
    slabs, modes = sizes
    chips_z, plane = modes // 2, slabs * 2
    rows, block = tensor_ref.shape[0], regrouped.shape[1]
    piece = plane_in.shape[1]
    slab, mode = lax.axis_index("slab"), lax.axis_index("mode")
    z, core = mode // 2, lax.rem(mode, 2)
    spot = slab * 2 + core

    def z_peer(dz, flip):
        peer_core = core if flip == 0 else 1 - core
        return lax.rem(z + dz + chips_z, chips_z) * 2 + peer_core

    def plane_peer(offset, sign=1):
        dy, dx, flip = offset
        row = lax.rem(slab // 4 + sign * dy + 4, 4)
        column = lax.rem(lax.rem(slab, 4) + sign * dx + 4, 4)
        return row * 4 + column, core if flip == 0 else 1 - core

    half = chips_z // 2
    order = [half]
    for distance in range(half - 1, 0, -1):
        order += [distance, -distance]
    z_steps = [(dz, flip) for dz in order for flip in (0, 1)] + [(0, 1)]
    side = 4
    x, y = lax.rem(slab, side), slab // side

    def hops(offset):
        return sum(min(d, side - d) for d in offset[:2])

    plane_steps = [(dy, dx, flip) for dy in range(side) for dx in range(side) for flip in (0, 1)][1:]
    plane_steps.sort(key=lambda offset: -hops(offset))
    x_beside = [(y * side + lax.rem(x + d, side), mode) for d in (1, side - 1)]
    y_beside = [(lax.rem(y + d, side) * side + x, mode) for d in (1, side - 1)]
    z_beside = [(slab, z_peer(dz, 0)) for dz in (1, -1)]
    other_core = (slab, z_peer(0, 1))

    def tell(semaphore, device):
        pl.semaphore_signal(semaphore, inc=1, device_id=device, device_id_type=MESH)

    barrier = pltpu.get_barrier_semaphore()
    beside = z_beside + [(slab, z_peer(dz, 1)) for dz in (1, -1)] + [other_core] + x_beside + y_beside
    for device in beside:
        tell(barrier, device)
    own = pltpu.make_async_copy(
        tensor_ref.at[:, pl.ds(pl.multiple_of(mode * block, block), block)],
        regrouped.at[pl.ds(pl.multiple_of(mode * rows, rows), rows), :],
        own_sem,
    )
    own.start()
    fetch = pltpu.make_async_copy(start_ref, start, start_sem)
    fetch.start()
    pl.semaphore_wait(barrier, len(beside))

    def a2a(index, dz, flip, landing):
        peer = z_peer(dz, flip)
        return pltpu.make_async_remote_copy(
            src_ref=tensor_ref.at[:, pl.ds(pl.multiple_of(peer * block, block), block)],
            dst_ref=regrouped.at[pl.ds(pl.multiple_of(landing * rows, rows), rows), :],
            send_sem=a2a_send.at[index],
            recv_sem=a2a_recv.at[index],
            device_id=(slab, peer),
            device_id_type=MESH,
        )

    def send(distances):
        for index, (dz, flip) in enumerate(z_steps):
            if dz in distances:
                a2a(index, dz, flip, mode).start()

    def reach(known, devices):
        for way in (0, 1):
            tell(known.at[way], devices[way])

    def heard(known):
        for way in (0, 1):
            pl.semaphore_wait(known.at[way], 1)

    reach(z_known.at[0], z_beside)
    reach(x_known, x_beside)
    send((1, -1, 0))
    for further in range(1, half):
        heard(z_known.at[further - 1])
        if further + 1 < half:
            reach(z_known.at[further], z_beside)
        if further == 1:
            send((2, -2))
    send([dz for dz in order if abs(dz) > 2])
    heard(x_known)
    tell(core_known, other_core)
    pl.semaphore_wait(core_known, 1)
    reach(y_known.at[0], y_beside)
    heard(y_known.at[0])
    reach(y_known.at[1], y_beside)
    heard(y_known.at[1])

    fetch.wait()
    start_t = start[...].T
    high = start_t.astype(BF16)
    split_start[0] = high
    split_start[1] = (start_t - high.astype(F32)).astype(BF16)

    own.wait()
    for index, (dz, flip) in enumerate(z_steps):
        a2a(index, dz, flip, z_peer(-dz, flip)).wait_recv()

    whole = regrouped[...]
    projected = jnp.dot(split_start[0], whole, preferred_element_type=F32)
    projected += jnp.dot(split_start[1], whole, preferred_element_type=F32)
    high = projected.astype(BF16)
    low = (projected - high.astype(F32)).astype(BF16)
    last = (((1,), (1,)), ((), ()))
    partial = lax.dot_general(whole, high, last, preferred_element_type=F32)
    partial += lax.dot_general(whole, low, last, preferred_element_type=F32)
    partial_low[...] = partial.astype(BF16).reshape(partial_low.shape)

    def scatter(index, offset, landing):
        other, peer_core = plane_peer(offset)
        return pltpu.make_async_remote_copy(
            src_ref=partial_low.at[other * 2 + peer_core],
            dst_ref=plane_in.at[landing],
            send_sem=rs_send.at[index],
            recv_sem=rs_recv.at[index],
            device_id=(other, z * 2 + peer_core),
            device_id_type=MESH,
        )

    for index, offset in enumerate(plane_steps):
        scatter(index, offset, spot).start()
    plane_in[spot] = partial_low[spot]
    turned_ref[...] = regrouped[...].T
    for index, offset in enumerate(plane_steps):
        other, peer_core = plane_peer(offset, -1)
        scatter(index, offset, other * 2 + peer_core).wait_recv()
    mine[...] = jnp.sum(plane_in[...].astype(F32), axis=0)
    z_in[z] = mine[...]

    def along_z(index, dz, landing):
        peer = z_peer(dz, 0)
        return pltpu.make_async_remote_copy(
            src_ref=mine,
            dst_ref=z_in.at[landing],
            send_sem=z_send.at[index],
            recv_sem=z_recv.at[index],
            device_id=(slab, peer),
            device_id_type=MESH,
        )

    for index, dz in enumerate(order):
        along_z(index, dz, z).start()
    for index, dz in enumerate(order):
        along_z(index, dz, lax.rem(z - dz + chips_z, chips_z)).wait_recv()
    image_ref[spot] = jnp.sum(z_in[...], axis=0)

    def gather(index, offset, landing):
        other, peer_core = plane_peer(offset)
        return pltpu.make_async_remote_copy(
            src_ref=image_ref.at[spot],
            dst_ref=image_ref.at[landing],
            send_sem=ag_send.at[index],
            recv_sem=ag_recv.at[index],
            device_id=(other, z * 2 + peer_core),
            device_id_type=MESH,
        )

    for index, offset in enumerate(plane_steps):
        gather(index, offset, spot).start()
    for index, offset in enumerate(plane_steps):
        other, peer_core = plane_peer(offset, -1)
        gather(index, offset, other * 2 + peer_core).wait_recv()

    for index, (dz, flip) in enumerate(z_steps):
        a2a(index, dz, flip, mode).wait_send()
    for index, offset in enumerate(plane_steps):
        scatter(index, offset, spot).wait_send()
        gather(index, offset, spot).wait_send()
    for index, dz in enumerate(order):
        along_z(index, dz, z).wait_send()


def inverse_factor(gram):
    n = gram.shape[0]
    tall = n // 8
    lane = lax.broadcasted_iota(jnp.int32, (8, n), 1)
    sub = lax.broadcasted_iota(jnp.int32, (8, n), 0)
    spread = lambda x, k: jnp.broadcast_to(x[:, k : k + 1], (8, n))
    pick = lambda x, k: jnp.broadcast_to(x[k : k + 1], (8, n))
    work = [gram[8 * r : 8 * r + 8, :] for r in range(tall)]
    out = []
    ahead = [spread(work[0], k) for k in range(8)]
    for p in range(tall):
        below = range(p, tall)
        cols = [{r: ahead[k] if r == p else spread(work[r], 8 * p + k) for r in below} for k in range(8)]
        if p + 1 < tall:
            ahead = [spread(work[p + 1], 8 * (p + 1) + k) for k in range(8)]
        done = jnp.zeros((8, n), F32)
        for s in range(0, 8, 2):
            j = 8 * p + s
            col_a, col_b = cols[s], cols[s + 1]
            a, b, c = pick(col_a[p], s), pick(col_a[p], s + 1), pick(col_b[p], s + 1)
            det = a * c - b * b
            inv = 1.0 / det
            ia, ib, ic = c * inv, b * inv, a * inv
            for k in range(s + 2, 8):
                va, vb = pick(col_a[p], k), pick(col_b[p], k)
                ta, tb = ia * va - ib * vb, ic * vb - ib * va
                for r in below:
                    cols[k][r] = cols[k][r] - (col_a[r] * ta + col_b[r] * tb)
            if p + 1 < tall:
                for k in range(8):
                    va, vb = pick(col_a[p + 1], k), pick(col_b[p + 1], k)
                    ta, tb = ia * va - ib * vb, ic * vb - ib * va
                    ahead[k] = ahead[k] - (col_a[p + 1] * ta + col_b[p + 1] * tb)
            row_a, row_b = pick(work[p], s), pick(work[p], s + 1)
            unit_a = jnp.where(lane == j, 1.0, 0.0).astype(F32)
            unit_b = jnp.where(lane == j + 1, 1.0, 0.0).astype(F32)
            full_a, full_b = row_a + unit_a, row_b + unit_b
            ta = ia * full_a - ib * full_b
            tb = ic * full_b - ib * full_a
            left_a = jnp.where(lane < j, row_a, unit_a)
            left_b = jnp.where(lane < j, row_b, unit_b)
            root_a = lax.rsqrt(a)
            root_b = lax.rsqrt(det * (root_a * root_a))
            w_a = left_a * root_a
            w_b = (left_b - (b * root_a) * w_a) * root_b
            done = jnp.where(sub == s, w_a, jnp.where(sub == s + 1, w_b, done))
            for r in below:
                work[r] = work[r] - (col_a[r] * ta + col_b[r] * tb)
        out.append(done)
    return jnp.concatenate(out, axis=0)


def finish(turned_ref, image_ref, rows_ref, core_ref, basis):
    image = image_ref[...].reshape(basis.shape)
    image = image * lax.rsqrt(jnp.sum(image * image, axis=0, keepdims=True))
    across = (((0,), (0,)), ((), ()))
    gram = lax.dot_general(image, image, across, precision=highest, preferred_element_type=F32)
    inverse = inverse_factor(gram)
    whole = lax.dot_general(
        image, inverse, (((1,), (1,)), ((), ())), precision=highest, preferred_element_type=F32
    )
    basis[...] = whole
    count = rows_ref.shape[0]
    rows_ref[...] = basis[pl.ds(pl.multiple_of(lax.axis_index("mode") * count, count), count), :]
    core_ref[...] = jnp.dot(turned_ref[...], whole.astype(BF16), preferred_element_type=F32)


def shards(sizes, tensor, start_block):
    slabs, modes = sizes
    rows, width = tensor.shape
    full, rank = start_block.shape
    block = width // modes
    plane = slabs * 2
    piece = full // plane
    dma, regular = pltpu.SemaphoreType.DMA, pltpu.SemaphoreType.REGULAR
    turned, image = pl.pallas_call(
        functools.partial(exchange, sizes),
        out_shape=(
            pltpu.VMEM((block, full), BF16),
            pltpu.VMEM((plane, piece, rank), F32),
        ),
        in_specs=[pl.BlockSpec(memory_space=pl.ANY)] * 2,
        out_specs=(pl.BlockSpec(memory_space=pltpu.VMEM), pl.BlockSpec(memory_space=pltpu.VMEM)),
        scratch_shapes=[
            pltpu.VMEM((full, rank), F32),
            pltpu.VMEM((full, block), BF16),
            pltpu.VMEM((2, rank, full), BF16),
            pltpu.VMEM((plane, piece, rank), BF16),
            pltpu.VMEM((plane, piece, rank), BF16),
            pltpu.VMEM((modes // 2, piece, rank), F32),
            pltpu.VMEM((piece, rank), F32),
            dma, dma,
            regular((modes // 4 - 1, 2)), regular((2,)), regular, regular((2, 2)),
            dma((modes,)), dma((modes,)),
            dma((plane,)), dma((plane,)),
            dma((modes // 2,)), dma((modes // 2,)),
            dma((plane,)), dma((plane,)),
        ],
        compiler_params=pltpu.CompilerParams(collective_id=0, has_side_effects=True),
        name="exchange",
    )(tensor, start_block)
    return pl.pallas_call(
        finish,
        out_shape=(
            jax.ShapeDtypeStruct((rows, rank), F32),
            jax.ShapeDtypeStruct((block, rank), F32),
        ),
        in_specs=[pl.BlockSpec(memory_space=pltpu.VMEM)] * 2,
        scratch_shapes=[pltpu.VMEM((full, rank), F32)],
        name="finish",
    )(*(pltpu.with_memory_space_constraint(x, pltpu.VMEM) for x in (turned, image)))


def solution(mesh):
    sizes = (mesh.shape["slab"], mesh.shape["mode"])
    return jax.shard_map(
        functools.partial(shards, sizes),
        mesh=mesh,
        in_specs=(P("mode", "slab"), P()),
        out_specs=(P("mode", None), P(("slab", "mode"), None)),
        check_vma=False,
    )
```

```python
import functools

import jax
import jax.numpy as jnp
from jax import lax
from jax.experimental import pallas as pl
from jax.experimental.pallas import tpu as pltpu
from jax.sharding import PartitionSpec as P

MESH = pl.DeviceIdType.MESH
highest = lax.Precision.HIGHEST
BF16, F32 = jnp.bfloat16, jnp.float32


def exchange(sizes, tensor_ref, start_ref, turned_ref, image_ref,
             start, regrouped, split_start, partial_low, plane_in, z_in, mine,
             start_sem, own_sem, z_known, x_known, core_known, y_known, a2a_send, a2a_recv, rs_send, rs_recv,
             z_send, z_recv, ag_send, ag_recv):
    slabs, modes = sizes
    chips_z, plane = modes // 2, slabs * 2
    rows, block = tensor_ref.shape[0], regrouped.shape[1]
    piece = plane_in.shape[1]
    slab, mode = lax.axis_index("slab"), lax.axis_index("mode")
    z, core = mode // 2, lax.rem(mode, 2)
    spot = slab * 2 + core

    def z_peer(dz, flip):
        peer_core = core if flip == 0 else 1 - core
        return lax.rem(z + dz + chips_z, chips_z) * 2 + peer_core

    def plane_peer(offset, sign=1):
        dy, dx, flip = offset
        row = lax.rem(slab // 4 + sign * dy + 4, 4)
        column = lax.rem(lax.rem(slab, 4) + sign * dx + 4, 4)
        return row * 4 + column, core if flip == 0 else 1 - core

    half = chips_z // 2
    order = [half]
    for distance in range(half - 1, 0, -1):
        order += [distance, -distance]
    z_steps = [(dz, flip) for dz in order for flip in (0, 1)] + [(0, 1)]
    side = 4
    x, y = lax.rem(slab, side), slab // side

    def hops(offset):
        return sum(min(d, side - d) for d in offset[:2])

    plane_steps = [(dy, dx, flip) for dy in range(side) for dx in range(side) for flip in (0, 1)][1:]
    plane_steps.sort(key=lambda offset: -hops(offset))
    x_beside = [(y * side + lax.rem(x + d, side), mode) for d in (1, side - 1)]
    y_beside = [(lax.rem(y + d, side) * side + x, mode) for d in (1, side - 1)]
    z_beside = [(slab, z_peer(dz, 0)) for dz in (1, -1)]
    other_core = (slab, z_peer(0, 1))

    def tell(semaphore, device):
        pl.semaphore_signal(semaphore, inc=1, device_id=device, device_id_type=MESH)

    barrier = pltpu.get_barrier_semaphore()
    beside = z_beside + [(slab, z_peer(dz, 1)) for dz in (1, -1)] + [other_core] + x_beside + y_beside
    for device in beside:
        tell(barrier, device)
    own = pltpu.make_async_copy(
        tensor_ref.at[:, pl.ds(pl.multiple_of(mode * block, block), block)],
        regrouped.at[pl.ds(pl.multiple_of(mode * rows, rows), rows), :],
        own_sem,
    )
    own.start()
    fetch = pltpu.make_async_copy(start_ref, start, start_sem)
    fetch.start()
    pl.semaphore_wait(barrier, len(beside))

    def a2a(index, dz, flip, landing):
        peer = z_peer(dz, flip)
        return pltpu.make_async_remote_copy(
            src_ref=tensor_ref.at[:, pl.ds(pl.multiple_of(peer * block, block), block)],
            dst_ref=regrouped.at[pl.ds(pl.multiple_of(landing * rows, rows), rows), :],
            send_sem=a2a_send.at[index],
            recv_sem=a2a_recv.at[index],
            device_id=(slab, peer),
            device_id_type=MESH,
        )

    def send(distances):
        for index, (dz, flip) in enumerate(z_steps):
            if dz in distances:
                a2a(index, dz, flip, mode).start()

    def reach(known, devices):
        for way in (0, 1):
            tell(known.at[way], devices[way])

    def heard(known):
        for way in (0, 1):
            pl.semaphore_wait(known.at[way], 1)

    reach(z_known.at[0], z_beside)
    reach(x_known, x_beside)
    send((1, -1, 0))
    for further in range(1, half):
        heard(z_known.at[further - 1])
        if further + 1 < half:
            reach(z_known.at[further], z_beside)
        if further == 1:
            send((2, -2))
    send([dz for dz in order if abs(dz) > 2])
    heard(x_known)
    tell(core_known, other_core)
    pl.semaphore_wait(core_known, 1)
    reach(y_known.at[0], y_beside)
    heard(y_known.at[0])
    reach(y_known.at[1], y_beside)
    heard(y_known.at[1])

    fetch.wait()
    start_t = start[...].T
    high = start_t.astype(BF16)
    rank = start.shape[1]
    split_start[:rank, :] = high
    split_start[rank:, :] = (start_t - high.astype(F32)).astype(BF16)

    own.wait()
    for index, (dz, flip) in enumerate(z_steps):
        a2a(index, dz, flip, z_peer(-dz, flip)).wait_recv()

    whole = regrouped[...]
    halves = jnp.dot(split_start[...], whole, preferred_element_type=F32)
    projected = halves[:rank] + halves[rank:]
    high = projected.astype(BF16)
    low = (projected - high.astype(F32)).astype(BF16)
    halves = lax.dot_general(
        whole, jnp.concatenate([high, low], axis=0), (((1,), (1,)), ((), ())), preferred_element_type=F32
    )
    partial = halves[:, :rank] + halves[:, rank:]
    partial_low[...] = partial.astype(BF16).reshape(partial_low.shape)

    def scatter(index, offset, landing):
        other, peer_core = plane_peer(offset)
        return pltpu.make_async_remote_copy(
            src_ref=partial_low.at[other * 2 + peer_core],
            dst_ref=plane_in.at[landing],
            send_sem=rs_send.at[index],
            recv_sem=rs_recv.at[index],
            device_id=(other, z * 2 + peer_core),
            device_id_type=MESH,
        )

    for index, offset in enumerate(plane_steps):
        scatter(index, offset, spot).start()
    plane_in[spot] = partial_low[spot]
    turned_ref[...] = regrouped[...].T
    for index, offset in enumerate(plane_steps):
        other, peer_core = plane_peer(offset, -1)
        scatter(index, offset, other * 2 + peer_core).wait_recv()
    mine[...] = jnp.sum(plane_in[...].astype(F32), axis=0)
    z_in[z] = mine[...]

    def along_z(index, dz, landing):
        peer = z_peer(dz, 0)
        return pltpu.make_async_remote_copy(
            src_ref=mine,
            dst_ref=z_in.at[landing],
            send_sem=z_send.at[index],
            recv_sem=z_recv.at[index],
            device_id=(slab, peer),
            device_id_type=MESH,
        )

    for index, dz in enumerate(order):
        along_z(index, dz, z).start()
    for index, dz in enumerate(order):
        along_z(index, dz, lax.rem(z - dz + chips_z, chips_z)).wait_recv()
    image_ref[spot] = jnp.sum(z_in[...], axis=0)

    def gather(index, offset, landing):
        other, peer_core = plane_peer(offset)
        return pltpu.make_async_remote_copy(
            src_ref=image_ref.at[spot],
            dst_ref=image_ref.at[landing],
            send_sem=ag_send.at[index],
            recv_sem=ag_recv.at[index],
            device_id=(other, z * 2 + peer_core),
            device_id_type=MESH,
        )

    for index, offset in enumerate(plane_steps):
        gather(index, offset, spot).start()
    for index, offset in enumerate(plane_steps):
        other, peer_core = plane_peer(offset, -1)
        gather(index, offset, other * 2 + peer_core).wait_recv()

    for index, (dz, flip) in enumerate(z_steps):
        a2a(index, dz, flip, mode).wait_send()
    for index, offset in enumerate(plane_steps):
        scatter(index, offset, spot).wait_send()
        gather(index, offset, spot).wait_send()
    for index, dz in enumerate(order):
        along_z(index, dz, z).wait_send()


def inverse_factor(gram):
    n = gram.shape[0]
    tall = n // 8
    lane = lax.broadcasted_iota(jnp.int32, (8, n), 1)
    sub = lax.broadcasted_iota(jnp.int32, (8, n), 0)
    spread = lambda x, k: jnp.broadcast_to(x[:, k : k + 1], (8, n))
    pick = lambda x, k: jnp.broadcast_to(x[k : k + 1], (8, n))
    work = [gram[8 * r : 8 * r + 8, :] for r in range(tall)]
    nothing = work[0] * 0.0
    ahead = [spread(work[0], k) + nothing for k in range(8)]
    out = []
    for p in range(tall):
        cols, more = ahead, p + 1 < tall
        far = {r: [spread(work[r], 8 * p + k) for k in range(8)] for r in range(p + 1, tall)}
        if more:
            beside = [x + nothing for x in far[p + 1]]
            ahead = [spread(work[p + 1], 8 * (p + 1) + k) for k in range(8)]
        rows = work[p]
        done = nothing
        for s in range(0, 8, 2):
            j = 8 * p + s
            col_a, col_b = cols[s], cols[s + 1]
            a, b, c = pick(col_a, s), pick(col_a, s + 1), pick(col_b, s + 1)
            det = a * c - b * b
            inv = 1.0 / det
            ia, ib, ic = c * inv, b * inv, a * inv
            mul_a, mul_b = ia * col_a - ib * col_b, ic * col_b - ib * col_a
            if more:
                next_a, next_b = beside[s], beside[s + 1]
                low_a, low_b = ia * next_a - ib * next_b, ic * next_b - ib * next_a
                for k in range(8):
                    ahead[k] = ahead[k] - (low_a * pick(next_a, k) + low_b * pick(next_b, k))
                for k in range(s + 2, 8):
                    beside[k] = beside[k] - (low_a * pick(cols[k], s) + low_b * pick(cols[k], s + 1))
            row_a, row_b = pick(rows, s), pick(rows, s + 1)
            unit_a = jnp.where(lane == j, 1.0, 0.0).astype(F32)
            unit_b = jnp.where(lane == j + 1, 1.0, 0.0).astype(F32)
            left_a = jnp.where(lane < j, row_a, unit_a)
            left_b = jnp.where(lane < j, row_b, unit_b)
            root_a = lax.rsqrt(a)
            root_b = lax.rsqrt(det * (root_a * root_a))
            w_a = left_a * root_a
            w_b = (left_b - (b * root_a) * w_a) * root_b
            done = jnp.where(sub == s, w_a, jnp.where(sub == s + 1, w_b, done))
            if s < 6:
                rows = jnp.where((lane == j) | (lane == j + 1), 0.0, rows) - (mul_a * left_a + mul_b * left_b)
            swept_a = jnp.where(sub == s, 1.0 - ia, jnp.where(sub == s + 1, ib, mul_a))
            swept_b = jnp.where(sub == s, ib, jnp.where(sub == s + 1, 1.0 - ic, mul_b))
            for k in range(8):
                if k < s or (k > s + 1):
                    if more or k > s + 1:
                        cols[k] = cols[k] - (swept_a * pick(cols[k], s) + swept_b * pick(cols[k], s + 1))
            cols[s] = jnp.where(sub == s, 1.0, 0.0) - swept_a
            cols[s + 1] = jnp.where(sub == s + 1, 1.0, 0.0) - swept_b
        out.append(done)
        if more:
            within = (lane >= 8 * p) & (lane < 8 * p + 8)
            terms = [
                cols[k] * jnp.where(within, jnp.where(lane == 8 * p + k, 1.0, 0.0), pick(work[p], k))
                for k in range(8)
            ]
            solved = ((terms[0] + terms[1]) + (terms[2] + terms[3])) + ((terms[4] + terms[5]) + (terms[6] + terms[7]))
            against = [pick(solved, k) for k in range(8)]
            for r in range(p + 1, tall):
                terms = [far[r][k] * against[k] for k in range(8)]
                total = ((terms[0] + terms[1]) + (terms[2] + terms[3])) + ((terms[4] + terms[5]) + (terms[6] + terms[7]))
                work[r] = jnp.where(within, 0.0, work[r]) - total
    return jnp.concatenate(out, axis=0)


def finish(turned_ref, image_ref, rows_ref, core_ref, basis):
    image = image_ref[...].reshape(basis.shape)
    image = image * lax.rsqrt(jnp.sum(image * image, axis=0, keepdims=True))
    across = (((0,), (0,)), ((), ()))
    gram = lax.dot_general(image, image, across, precision=highest, preferred_element_type=F32)
    inverse = inverse_factor(gram)
    whole = lax.dot_general(
        image, inverse, (((1,), (1,)), ((), ())), precision=highest, preferred_element_type=F32
    )
    basis[...] = whole
    count = rows_ref.shape[0]
    rows_ref[...] = basis[pl.ds(pl.multiple_of(lax.axis_index("mode") * count, count), count), :]
    core_ref[...] = jnp.dot(turned_ref[...], whole.astype(BF16), preferred_element_type=F32)


def shards(sizes, tensor, start_block):
    slabs, modes = sizes
    rows, width = tensor.shape
    full, rank = start_block.shape
    block = width // modes
    plane = slabs * 2
    piece = full // plane
    dma, regular = pltpu.SemaphoreType.DMA, pltpu.SemaphoreType.REGULAR
    turned, image = pl.pallas_call(
        functools.partial(exchange, sizes),
        out_shape=(
            pltpu.VMEM((block, full), BF16),
            pltpu.VMEM((plane, piece, rank), F32),
        ),
        in_specs=[pl.BlockSpec(memory_space=pl.ANY)] * 2,
        out_specs=(pl.BlockSpec(memory_space=pltpu.VMEM), pl.BlockSpec(memory_space=pltpu.VMEM)),
        scratch_shapes=[
            pltpu.VMEM((full, rank), F32),
            pltpu.VMEM((full, block), BF16),
            pltpu.VMEM((2 * rank, full), BF16),
            pltpu.VMEM((plane, piece, rank), BF16),
            pltpu.VMEM((plane, piece, rank), BF16),
            pltpu.VMEM((modes // 2, piece, rank), F32),
            pltpu.VMEM((piece, rank), F32),
            dma, dma,
            regular((modes // 4 - 1, 2)), regular((2,)), regular, regular((2, 2)),
            dma((modes,)), dma((modes,)),
            dma((plane,)), dma((plane,)),
            dma((modes // 2,)), dma((modes // 2,)),
            dma((plane,)), dma((plane,)),
        ],
        compiler_params=pltpu.CompilerParams(collective_id=0, has_side_effects=True),
        name="exchange",
    )(tensor, start_block)
    return pl.pallas_call(
        finish,
        out_shape=(
            jax.ShapeDtypeStruct((rows, rank), F32),
            jax.ShapeDtypeStruct((block, rank), F32),
        ),
        in_specs=[pl.BlockSpec(memory_space=pltpu.VMEM)] * 2,
        scratch_shapes=[pltpu.VMEM((full, rank), F32)],
        name="finish",
    )(*(pltpu.with_memory_space_constraint(x, pltpu.VMEM) for x in (turned, image)))


def solution(mesh):
    sizes = (mesh.shape["slab"], mesh.shape["mode"])
    return jax.shard_map(
        functools.partial(shards, sizes),
        mesh=mesh,
        in_specs=(P("mode", "slab"), P()),
        out_specs=(P("mode", None), P(("slab", "mode"), None)),
        check_vma=False,
    )
```

```python
import functools

import jax
import jax.numpy as jnp
from jax import lax
from jax.experimental import pallas as pl
from jax.experimental.pallas import tpu as pltpu
from jax.sharding import PartitionSpec as P

MESH = pl.DeviceIdType.MESH
highest = lax.Precision.HIGHEST
BF16, F32 = jnp.bfloat16, jnp.float32


def exchange(sizes, tensor_ref, start_ref, turned_ref, image_ref,
             start, regrouped, split_start, partial_low, plane_in, z_in, mine,
             start_sem, own_sem, z_known, x_known, core_known, y_known, a2a_send, a2a_recv, rs_send, rs_recv,
             z_send, z_recv, ag_send, ag_recv):
    slabs, modes = sizes
    chips_z, plane = modes // 2, slabs * 2
    rows, block = tensor_ref.shape[0], regrouped.shape[1]
    piece = plane_in.shape[1]
    slab, mode = lax.axis_index("slab"), lax.axis_index("mode")
    z, core = mode // 2, lax.rem(mode, 2)
    spot = slab * 2 + core

    def z_peer(dz, flip):
        peer_core = core if flip == 0 else 1 - core
        return lax.rem(z + dz + chips_z, chips_z) * 2 + peer_core

    def plane_peer(offset, sign=1):
        dy, dx, flip = offset
        row = lax.rem(slab // 4 + sign * dy + 4, 4)
        column = lax.rem(lax.rem(slab, 4) + sign * dx + 4, 4)
        return row * 4 + column, core if flip == 0 else 1 - core

    half = chips_z // 2
    order = [half]
    for distance in range(half - 1, 0, -1):
        order += [distance, -distance]
    z_steps = [(dz, flip) for dz in order for flip in (0, 1)] + [(0, 1)]
    side = 4
    x, y = lax.rem(slab, side), slab // side

    def hops(offset):
        return sum(min(d, side - d) for d in offset[:2])

    plane_steps = [(dy, dx, flip) for dy in range(side) for dx in range(side) for flip in (0, 1)][1:]
    plane_steps.sort(key=lambda offset: -hops(offset))
    x_beside = [(y * side + lax.rem(x + d, side), mode) for d in (1, side - 1)]
    y_beside = [(lax.rem(y + d, side) * side + x, mode) for d in (1, side - 1)]
    z_beside = [(slab, z_peer(dz, 0)) for dz in (1, -1)]
    other_core = (slab, z_peer(0, 1))

    def tell(semaphore, device):
        pl.semaphore_signal(semaphore, inc=1, device_id=device, device_id_type=MESH)

    barrier = pltpu.get_barrier_semaphore()
    beside = z_beside + [(slab, z_peer(dz, 1)) for dz in (1, -1)] + [other_core] + x_beside + y_beside
    for device in beside:
        tell(barrier, device)
    own = pltpu.make_async_copy(
        tensor_ref.at[:, pl.ds(pl.multiple_of(mode * block, block), block)],
        regrouped.at[pl.ds(pl.multiple_of(mode * rows, rows), rows), :],
        own_sem,
    )
    own.start()
    fetch = pltpu.make_async_copy(start_ref, start, start_sem)
    fetch.start()
    pl.semaphore_wait(barrier, len(beside))

    def a2a(index, dz, flip, landing):
        peer = z_peer(dz, flip)
        return pltpu.make_async_remote_copy(
            src_ref=tensor_ref.at[:, pl.ds(pl.multiple_of(peer * block, block), block)],
            dst_ref=regrouped.at[pl.ds(pl.multiple_of(landing * rows, rows), rows), :],
            send_sem=a2a_send.at[index],
            recv_sem=a2a_recv.at[index],
            device_id=(slab, peer),
            device_id_type=MESH,
        )

    def send(distances):
        for index, (dz, flip) in enumerate(z_steps):
            if dz in distances:
                a2a(index, dz, flip, mode).start()

    def reach(known, devices):
        for way in (0, 1):
            tell(known.at[way], devices[way])

    def heard(known):
        for way in (0, 1):
            pl.semaphore_wait(known.at[way], 1)

    reach(z_known.at[0], z_beside)
    reach(x_known, x_beside)
    send((1, -1, 0))
    for further in range(1, half):
        heard(z_known.at[further - 1])
        if further + 1 < half:
            reach(z_known.at[further], z_beside)
        if further == 1:
            send((2, -2))
    send([dz for dz in order if abs(dz) > 2])
    heard(x_known)
    tell(core_known, other_core)
    pl.semaphore_wait(core_known, 1)
    reach(y_known.at[0], y_beside)
    heard(y_known.at[0])
    reach(y_known.at[1], y_beside)
    heard(y_known.at[1])

    fetch.wait()
    start_t = start[...].T
    high = start_t.astype(BF16)
    rank = start.shape[1]
    split_start[:rank, :] = high
    split_start[rank:, :] = (start_t - high.astype(F32)).astype(BF16)

    own.wait()
    for index, (dz, flip) in enumerate(z_steps):
        a2a(index, dz, flip, z_peer(-dz, flip)).wait_recv()

    whole = regrouped[...]
    half = whole.shape[1] // 2
    projected = []
    for columns in (whole[:, :half], whole[:, half:]):
        halves = jnp.dot(split_start[...], columns, preferred_element_type=F32)
        projected.append(halves[:rank] + halves[rank:])
    projected = jnp.concatenate(projected, axis=1)
    high = projected.astype(BF16)
    low = (projected - high.astype(F32)).astype(BF16)
    both = jnp.concatenate([high, low], axis=0)
    share = whole.shape[0] // 2
    for part in range(2):
        halves = lax.dot_general(
            whole[part * share : (part + 1) * share], both, (((1,), (1,)), ((), ())), preferred_element_type=F32
        )
        partial = halves[:, :rank] + halves[:, rank:]
        pieces = partial_low.shape[0] // 2
        partial_low[part * pieces : (part + 1) * pieces] = partial.astype(BF16).reshape(
            (pieces,) + partial_low.shape[1:]
        )

    def scatter(index, offset, landing):
        other, peer_core = plane_peer(offset)
        return pltpu.make_async_remote_copy(
            src_ref=partial_low.at[other * 2 + peer_core],
            dst_ref=plane_in.at[landing],
            send_sem=rs_send.at[index],
            recv_sem=rs_recv.at[index],
            device_id=(other, z * 2 + peer_core),
            device_id_type=MESH,
        )

    for index, offset in enumerate(plane_steps):
        scatter(index, offset, spot).start()
    plane_in[spot] = partial_low[spot]
    turned_ref[...] = regrouped[...].T
    for index, (dz, flip) in enumerate(z_steps):
        a2a(index, dz, flip, mode).wait_send()
    for index, offset in reversed(list(enumerate(plane_steps))):
        other, peer_core = plane_peer(offset, -1)
        scatter(index, offset, other * 2 + peer_core).wait_recv()
    mine[...] = jnp.sum(plane_in[...].astype(F32), axis=0)
    z_in[z] = mine[...]

    def along_z(index, dz, landing):
        peer = z_peer(dz, 0)
        return pltpu.make_async_remote_copy(
            src_ref=mine,
            dst_ref=z_in.at[landing],
            send_sem=z_send.at[index],
            recv_sem=z_recv.at[index],
            device_id=(slab, peer),
            device_id_type=MESH,
        )

    for index, dz in enumerate(order):
        along_z(index, dz, z).start()
    for index, offset in enumerate(plane_steps):
        scatter(index, offset, spot).wait_send()
    for index, dz in reversed(list(enumerate(order))):
        along_z(index, dz, lax.rem(z - dz + chips_z, chips_z)).wait_recv()
    image_ref[spot] = jnp.sum(z_in[...], axis=0)

    def gather(index, offset, landing):
        other, peer_core = plane_peer(offset)
        return pltpu.make_async_remote_copy(
            src_ref=image_ref.at[spot],
            dst_ref=image_ref.at[landing],
            send_sem=ag_send.at[index],
            recv_sem=ag_recv.at[index],
            device_id=(other, z * 2 + peer_core),
            device_id_type=MESH,
        )

    for index, offset in enumerate(plane_steps):
        gather(index, offset, spot).start()
    for index, dz in enumerate(order):
        along_z(index, dz, z).wait_send()
    for index, offset in enumerate(plane_steps):
        gather(index, offset, spot).wait_send()
    for index, offset in reversed(list(enumerate(plane_steps))):
        other, peer_core = plane_peer(offset, -1)
        gather(index, offset, other * 2 + peer_core).wait_recv()


def inverse_factor(gram):
    n = gram.shape[0]
    tall = n // 8
    lane = lax.broadcasted_iota(jnp.int32, (8, n), 1)
    sub = lax.broadcasted_iota(jnp.int32, (8, n), 0)
    spread = lambda x, k: jnp.broadcast_to(x[:, k : k + 1], (8, n))
    pick = lambda x, k: jnp.broadcast_to(x[k : k + 1], (8, n))
    work = [gram[8 * r : 8 * r + 8, :] for r in range(tall)]
    nothing = work[0] * 0.0
    ahead = [spread(work[0], k) + nothing for k in range(8)]
    out = []
    for p in range(tall):
        cols, more = ahead, p + 1 < tall
        far = {r: [spread(work[r], 8 * p + k) for k in range(8)] for r in range(p + 1, tall)}
        if more:
            beside = [x + nothing for x in far[p + 1]]
            ahead = [spread(work[p + 1], 8 * (p + 1) + k) for k in range(8)]
        rows = work[p]
        done = nothing
        for s in range(0, 8, 2):
            j = 8 * p + s
            col_a, col_b = cols[s], cols[s + 1]
            a, b, c = pick(col_a, s), pick(col_a, s + 1), pick(col_b, s + 1)
            det = a * c - b * b
            inv = 1.0 / det
            ia, ib, ic = c * inv, b * inv, a * inv
            mul_a, mul_b = ia * col_a - ib * col_b, ic * col_b - ib * col_a
            if more:
                next_a, next_b = beside[s], beside[s + 1]
                low_a, low_b = ia * next_a - ib * next_b, ic * next_b - ib * next_a
                for k in range(8):
                    ahead[k] = ahead[k] - (low_a * pick(next_a, k) + low_b * pick(next_b, k))
                for k in range(s + 2, 8):
                    beside[k] = beside[k] - (low_a * pick(cols[k], s) + low_b * pick(cols[k], s + 1))
            row_a, row_b = pick(rows, s), pick(rows, s + 1)
            unit_a = jnp.where(lane == j, 1.0, 0.0).astype(F32)
            unit_b = jnp.where(lane == j + 1, 1.0, 0.0).astype(F32)
            left_a = jnp.where(lane < j, row_a, unit_a)
            left_b = jnp.where(lane < j, row_b, unit_b)
            root_a = lax.rsqrt(a)
            root_b = lax.rsqrt(det * (root_a * root_a))
            w_a = left_a * root_a
            w_b = (left_b - (b * root_a) * w_a) * root_b
            done = jnp.where(sub == s, w_a, jnp.where(sub == s + 1, w_b, done))
            if s < 6:
                rows = jnp.where((lane == j) | (lane == j + 1), 0.0, rows) - (mul_a * left_a + mul_b * left_b)
            swept_a = jnp.where(sub == s, 1.0 - ia, jnp.where(sub == s + 1, ib, mul_a))
            swept_b = jnp.where(sub == s, ib, jnp.where(sub == s + 1, 1.0 - ic, mul_b))
            for k in range(8):
                if k < s or (k > s + 1):
                    if more or k > s + 1:
                        cols[k] = cols[k] - (swept_a * pick(cols[k], s) + swept_b * pick(cols[k], s + 1))
            cols[s] = jnp.where(sub == s, 1.0, 0.0) - swept_a
            cols[s + 1] = jnp.where(sub == s + 1, 1.0, 0.0) - swept_b
        out.append(done)
        if more:
            within = (lane >= 8 * p) & (lane < 8 * p + 8)
            terms = [
                cols[k] * jnp.where(within, jnp.where(lane == 8 * p + k, 1.0, 0.0), pick(work[p], k))
                for k in range(8)
            ]
            solved = ((terms[0] + terms[1]) + (terms[2] + terms[3])) + ((terms[4] + terms[5]) + (terms[6] + terms[7]))
            against = [pick(solved, k) for k in range(8)]
            for r in range(p + 1, tall):
                terms = [far[r][k] * against[k] for k in range(8)]
                total = ((terms[0] + terms[1]) + (terms[2] + terms[3])) + ((terms[4] + terms[5]) + (terms[6] + terms[7]))
                work[r] = jnp.where(within, 0.0, work[r]) - total
    return jnp.concatenate(out, axis=0)


def finish(turned_ref, image_ref, rows_ref, core_ref, basis):
    image = image_ref[...].reshape(basis.shape)
    image = image * lax.rsqrt(jnp.sum(image * image, axis=0, keepdims=True))
    across = (((0,), (0,)), ((), ()))
    half = image.shape[0] // 2
    gram = sum(
        lax.dot_general(rows, rows, across, precision=highest, preferred_element_type=F32)
        for rows in (image[:half], image[half:])
    )
    inverse = inverse_factor(gram)
    whole = jnp.concatenate(
        [
            lax.dot_general(
                rows, inverse, (((1,), (1,)), ((), ())), precision=highest, preferred_element_type=F32
            )
            for rows in (image[:half], image[half:])
        ],
        axis=0,
    )
    basis[...] = whole
    count = rows_ref.shape[0]
    rows_ref[...] = basis[pl.ds(pl.multiple_of(lax.axis_index("mode") * count, count), count), :]
    core_ref[...] = jnp.dot(turned_ref[...], whole.astype(BF16), preferred_element_type=F32)


def shards(sizes, tensor, start_block):
    slabs, modes = sizes
    rows, width = tensor.shape
    full, rank = start_block.shape
    block = width // modes
    plane = slabs * 2
    piece = full // plane
    dma, regular = pltpu.SemaphoreType.DMA, pltpu.SemaphoreType.REGULAR
    turned, image = pl.pallas_call(
        functools.partial(exchange, sizes),
        out_shape=(
            pltpu.VMEM((block, full), BF16),
            pltpu.VMEM((plane, piece, rank), F32),
        ),
        in_specs=[pl.BlockSpec(memory_space=pl.ANY)] * 2,
        out_specs=(pl.BlockSpec(memory_space=pltpu.VMEM), pl.BlockSpec(memory_space=pltpu.VMEM)),
        scratch_shapes=[
            pltpu.VMEM((full, rank), F32),
            pltpu.VMEM((full, block), BF16),
            pltpu.VMEM((2 * rank, full), BF16),
            pltpu.VMEM((plane, piece, rank), BF16),
            pltpu.VMEM((plane, piece, rank), BF16),
            pltpu.VMEM((modes // 2, piece, rank), F32),
            pltpu.VMEM((piece, rank), F32),
            dma, dma,
            regular((modes // 4 - 1, 2)), regular((2,)), regular, regular((2, 2)),
            dma((modes,)), dma((modes,)),
            dma((plane,)), dma((plane,)),
            dma((modes // 2,)), dma((modes // 2,)),
            dma((plane,)), dma((plane,)),
        ],
        compiler_params=pltpu.CompilerParams(collective_id=0, has_side_effects=True),
        name="exchange",
    )(tensor, start_block)
    return pl.pallas_call(
        finish,
        out_shape=(
            jax.ShapeDtypeStruct((rows, rank), F32),
            jax.ShapeDtypeStruct((block, rank), F32),
        ),
        in_specs=[pl.BlockSpec(memory_space=pltpu.VMEM)] * 2,
        scratch_shapes=[pltpu.VMEM((full, rank), F32)],
        name="finish",
    )(*(pltpu.with_memory_space_constraint(x, pltpu.VMEM) for x in (turned, image)))


def solution(mesh):
    sizes = (mesh.shape["slab"], mesh.shape["mode"])
    return jax.shard_map(
        functools.partial(shards, sizes),
        mesh=mesh,
        in_specs=(P("mode", "slab"), P()),
        out_specs=(P("mode", None), P(("slab", "mode"), None)),
        check_vma=False,
    )
```

```python
import functools

import jax
import jax.numpy as jnp
from jax import lax
from jax.experimental import pallas as pl
from jax.experimental.pallas import tpu as pltpu
from jax.sharding import PartitionSpec as P

MESH = pl.DeviceIdType.MESH
highest = lax.Precision.HIGHEST
BF16, F32 = jnp.bfloat16, jnp.float32


def exchange(sizes, tensor_ref, start_ref, turned_ref, image_ref,
             start, regrouped, split_start, partial_low, plane_in, z_in, mine,
             start_sem, own_sem, z_known, x_known, core_known, y_known, a2a_send, a2a_recv, rs_send, rs_recv,
             z_send, z_recv, ag_send, ag_recv):
    slabs, modes = sizes
    chips_z, plane = modes // 2, slabs * 2
    rows, block = tensor_ref.shape[0], regrouped.shape[1]
    piece = plane_in.shape[1]
    slab, mode = lax.axis_index("slab"), lax.axis_index("mode")
    z, core = mode // 2, lax.rem(mode, 2)
    spot = slab * 2 + core

    def z_peer(dz, flip):
        peer_core = core if flip == 0 else 1 - core
        return lax.rem(z + dz + chips_z, chips_z) * 2 + peer_core

    def plane_peer(offset, sign=1):
        dy, dx, flip = offset
        row = lax.rem(slab // 4 + sign * dy + 4, 4)
        column = lax.rem(lax.rem(slab, 4) + sign * dx + 4, 4)
        return row * 4 + column, core if flip == 0 else 1 - core

    half = chips_z // 2
    order = [half]
    for distance in range(half - 1, 0, -1):
        order += [distance, -distance]
    z_steps = [(dz, flip) for dz in order for flip in (0, 1)] + [(0, 1)]
    side = 4
    x, y = lax.rem(slab, side), slab // side

    def hops(offset):
        return sum(min(d, side - d) for d in offset[:2])

    plane_steps = [(dy, dx, flip) for dy in range(side) for dx in range(side) for flip in (0, 1)][1:]
    plane_steps.sort(key=lambda offset: -hops(offset))
    x_beside = [(y * side + lax.rem(x + d, side), mode) for d in (1, side - 1)]
    y_beside = [(lax.rem(y + d, side) * side + x, mode) for d in (1, side - 1)]
    z_beside = [(slab, z_peer(dz, 0)) for dz in (1, -1)]
    other_core = (slab, z_peer(0, 1))

    def tell(semaphore, device):
        pl.semaphore_signal(semaphore, inc=1, device_id=device, device_id_type=MESH)

    barrier = pltpu.get_barrier_semaphore()
    beside = z_beside + [(slab, z_peer(dz, 1)) for dz in (1, -1)] + [other_core] + x_beside + y_beside
    for device in beside:
        tell(barrier, device)
    own = pltpu.make_async_copy(
        tensor_ref.at[:, pl.ds(pl.multiple_of(mode * block, block), block)],
        regrouped.at[pl.ds(pl.multiple_of(mode * rows, rows), rows), :],
        own_sem,
    )
    own.start()
    fetch = pltpu.make_async_copy(start_ref, start, start_sem)
    fetch.start()
    pl.semaphore_wait(barrier, len(beside))

    def target(dz, flip):
        return z_peer(dz * (1 - 2 * core), flip)

    def source(dz, flip):
        sender = core if flip == 0 else 1 - core
        return z_peer(-dz * (1 - 2 * sender), flip)

    def a2a(index, dz, flip, landing):
        peer = target(dz, flip)
        return pltpu.make_async_remote_copy(
            src_ref=tensor_ref.at[:, pl.ds(pl.multiple_of(peer * block, block), block)],
            dst_ref=regrouped.at[pl.ds(pl.multiple_of(landing * rows, rows), rows), :],
            send_sem=a2a_send.at[index],
            recv_sem=a2a_recv.at[index],
            device_id=(slab, peer),
            device_id_type=MESH,
        )

    def send(distances):
        for index, (dz, flip) in enumerate(z_steps):
            if dz in distances:
                a2a(index, dz, flip, mode).start()

    def reach(known, devices):
        for way in (0, 1):
            tell(known.at[way], devices[way])

    def heard(known):
        for way in (0, 1):
            pl.semaphore_wait(known.at[way], 1)

    reach(z_known.at[0], z_beside)
    reach(x_known, x_beside)
    send((1, -1, 0))
    for further in range(1, half):
        heard(z_known.at[further - 1])
        if further + 1 < half:
            reach(z_known.at[further], z_beside)
        if further == 1:
            send((2, -2))
    send([dz for dz in order if abs(dz) > 2])
    heard(x_known)
    tell(core_known, other_core)
    pl.semaphore_wait(core_known, 1)
    reach(y_known.at[0], y_beside)
    heard(y_known.at[0])
    reach(y_known.at[1], y_beside)
    heard(y_known.at[1])

    fetch.wait()
    start_t = start[...].T
    high = start_t.astype(BF16)
    rank = start.shape[1]
    split_start[:rank, :] = high
    split_start[rank:, :] = (start_t - high.astype(F32)).astype(BF16)

    own.wait()
    for index, (dz, flip) in enumerate(z_steps):
        a2a(index, dz, flip, source(dz, flip)).wait_recv()

    whole = regrouped[...]
    half = whole.shape[1] // 2
    projected = []
    for columns in (whole[:, :half], whole[:, half:]):
        halves = jnp.dot(split_start[...], columns, preferred_element_type=F32)
        projected.append(halves[:rank] + halves[rank:])
    projected = jnp.concatenate(projected, axis=1)
    high = projected.astype(BF16)
    low = (projected - high.astype(F32)).astype(BF16)
    both = jnp.concatenate([high, low], axis=0)
    share = whole.shape[0] // 2
    for part in range(2):
        halves = lax.dot_general(
            whole[part * share : (part + 1) * share], both, (((1,), (1,)), ((), ())), preferred_element_type=F32
        )
        partial = halves[:, :rank] + halves[:, rank:]
        pieces = partial_low.shape[0] // 2
        partial_low[part * pieces : (part + 1) * pieces] = partial.astype(BF16).reshape(
            (pieces,) + partial_low.shape[1:]
        )

    def scatter(index, offset, landing):
        other, peer_core = plane_peer(offset)
        return pltpu.make_async_remote_copy(
            src_ref=partial_low.at[other * 2 + peer_core],
            dst_ref=plane_in.at[landing],
            send_sem=rs_send.at[index],
            recv_sem=rs_recv.at[index],
            device_id=(other, z * 2 + peer_core),
            device_id_type=MESH,
        )

    for index, offset in enumerate(plane_steps):
        scatter(index, offset, spot).start()
    plane_in[spot] = partial_low[spot]
    turned_ref[...] = regrouped[...].T
    for index, (dz, flip) in enumerate(z_steps):
        a2a(index, dz, flip, mode).wait_send()
    for index, offset in reversed(list(enumerate(plane_steps))):
        other, peer_core = plane_peer(offset, -1)
        scatter(index, offset, other * 2 + peer_core).wait_recv()
    mine[...] = jnp.sum(plane_in[...].astype(F32), axis=0)
    z_in[z] = mine[...]

    def along_z(index, dz, landing):
        peer = target(dz, 0)
        return pltpu.make_async_remote_copy(
            src_ref=mine,
            dst_ref=z_in.at[landing],
            send_sem=z_send.at[index],
            recv_sem=z_recv.at[index],
            device_id=(slab, peer),
            device_id_type=MESH,
        )

    for index, dz in enumerate(order):
        along_z(index, dz, z).start()
    for index, offset in enumerate(plane_steps):
        scatter(index, offset, spot).wait_send()
    for index, dz in reversed(list(enumerate(order))):
        along_z(index, dz, source(dz, 0) // 2).wait_recv()
    image_ref[spot] = jnp.sum(z_in[...], axis=0)

    def gather(index, offset, landing):
        other, peer_core = plane_peer(offset)
        return pltpu.make_async_remote_copy(
            src_ref=image_ref.at[spot],
            dst_ref=image_ref.at[landing],
            send_sem=ag_send.at[index],
            recv_sem=ag_recv.at[index],
            device_id=(other, z * 2 + peer_core),
            device_id_type=MESH,
        )

    for index, offset in enumerate(plane_steps):
        gather(index, offset, spot).start()
    for index, dz in enumerate(order):
        along_z(index, dz, z).wait_send()
    for index, offset in enumerate(plane_steps):
        gather(index, offset, spot).wait_send()
    for index, offset in reversed(list(enumerate(plane_steps))):
        other, peer_core = plane_peer(offset, -1)
        gather(index, offset, other * 2 + peer_core).wait_recv()


def inverse_factor(gram):
    n = gram.shape[0]
    tall = n // 8
    lane = lax.broadcasted_iota(jnp.int32, (8, n), 1)
    sub = lax.broadcasted_iota(jnp.int32, (8, n), 0)
    spread = lambda x, k: jnp.broadcast_to(x[:, k : k + 1], (8, n))
    pick = lambda x, k: jnp.broadcast_to(x[k : k + 1], (8, n))
    work = [gram[8 * r : 8 * r + 8, :] for r in range(tall)]
    nothing = work[0] * 0.0
    ahead = [spread(work[0], k) + nothing for k in range(8)]
    out = []
    for p in range(tall):
        cols, more = ahead, p + 1 < tall
        far = {r: [spread(work[r], 8 * p + k) for k in range(8)] for r in range(p + 1, tall)}
        if more:
            beside = [x + nothing for x in far[p + 1]]
            ahead = [spread(work[p + 1], 8 * (p + 1) + k) for k in range(8)]
        rows = work[p]
        done = nothing
        for s in range(0, 8, 2):
            j = 8 * p + s
            col_a, col_b = cols[s], cols[s + 1]
            a, b, c = pick(col_a, s), pick(col_a, s + 1), pick(col_b, s + 1)
            det = a * c - b * b
            inv = 1.0 / det
            ia, ib, ic = c * inv, b * inv, a * inv
            mul_a, mul_b = ia * col_a - ib * col_b, ic * col_b - ib * col_a
            if more:
                next_a, next_b = beside[s], beside[s + 1]
                low_a, low_b = ia * next_a - ib * next_b, ic * next_b - ib * next_a
                for k in range(8):
                    ahead[k] = ahead[k] - (low_a * pick(next_a, k) + low_b * pick(next_b, k))
                for k in range(s + 2, 8):
                    beside[k] = beside[k] - (low_a * pick(cols[k], s) + low_b * pick(cols[k], s + 1))
            row_a, row_b = pick(rows, s), pick(rows, s + 1)
            unit_a = jnp.where(lane == j, 1.0, 0.0).astype(F32)
            unit_b = jnp.where(lane == j + 1, 1.0, 0.0).astype(F32)
            left_a = jnp.where(lane < j, row_a, unit_a)
            left_b = jnp.where(lane < j, row_b, unit_b)
            root_a = lax.rsqrt(a)
            root_b = lax.rsqrt(det * (root_a * root_a))
            w_a = left_a * root_a
            w_b = (left_b - (b * root_a) * w_a) * root_b
            done = jnp.where(sub == s, w_a, jnp.where(sub == s + 1, w_b, done))
            if s < 6:
                rows = jnp.where((lane == j) | (lane == j + 1), 0.0, rows) - (mul_a * left_a + mul_b * left_b)
            swept_a = jnp.where(sub == s, 1.0 - ia, jnp.where(sub == s + 1, ib, mul_a))
            swept_b = jnp.where(sub == s, ib, jnp.where(sub == s + 1, 1.0 - ic, mul_b))
            for k in range(8):
                if k < s or (k > s + 1):
                    if more or k > s + 1:
                        cols[k] = cols[k] - (swept_a * pick(cols[k], s) + swept_b * pick(cols[k], s + 1))
            cols[s] = jnp.where(sub == s, 1.0, 0.0) - swept_a
            cols[s + 1] = jnp.where(sub == s + 1, 1.0, 0.0) - swept_b
        out.append(done)
        if more:
            within = (lane >= 8 * p) & (lane < 8 * p + 8)
            terms = [
                cols[k] * jnp.where(within, jnp.where(lane == 8 * p + k, 1.0, 0.0), pick(work[p], k))
                for k in range(8)
            ]
            solved = ((terms[0] + terms[1]) + (terms[2] + terms[3])) + ((terms[4] + terms[5]) + (terms[6] + terms[7]))
            against = [pick(solved, k) for k in range(8)]
            for r in range(p + 1, tall):
                terms = [far[r][k] * against[k] for k in range(8)]
                total = ((terms[0] + terms[1]) + (terms[2] + terms[3])) + ((terms[4] + terms[5]) + (terms[6] + terms[7]))
                work[r] = jnp.where(within, 0.0, work[r]) - total
    return jnp.concatenate(out, axis=0)


def finish(turned_ref, image_ref, rows_ref, core_ref, basis):
    image = image_ref[...].reshape(basis.shape)
    image = image * lax.rsqrt(jnp.sum(image * image, axis=0, keepdims=True))
    across = (((0,), (0,)), ((), ()))
    half = image.shape[0] // 2
    gram = sum(
        lax.dot_general(rows, rows, across, precision=highest, preferred_element_type=F32)
        for rows in (image[:half], image[half:])
    )
    inverse = inverse_factor(gram)
    whole = jnp.concatenate(
        [
            lax.dot_general(
                rows, inverse, (((1,), (1,)), ((), ())), precision=highest, preferred_element_type=F32
            )
            for rows in (image[:half], image[half:])
        ],
        axis=0,
    )
    basis[...] = whole
    count = rows_ref.shape[0]
    rows_ref[...] = basis[pl.ds(pl.multiple_of(lax.axis_index("mode") * count, count), count), :]
    core_ref[...] = jnp.dot(turned_ref[...], whole.astype(BF16), preferred_element_type=F32)


def shards(sizes, tensor, start_block):
    slabs, modes = sizes
    rows, width = tensor.shape
    full, rank = start_block.shape
    block = width // modes
    plane = slabs * 2
    piece = full // plane
    dma, regular = pltpu.SemaphoreType.DMA, pltpu.SemaphoreType.REGULAR
    turned, image = pl.pallas_call(
        functools.partial(exchange, sizes),
        out_shape=(
            pltpu.VMEM((block, full), BF16),
            pltpu.VMEM((plane, piece, rank), F32),
        ),
        in_specs=[pl.BlockSpec(memory_space=pl.ANY)] * 2,
        out_specs=(pl.BlockSpec(memory_space=pltpu.VMEM), pl.BlockSpec(memory_space=pltpu.VMEM)),
        scratch_shapes=[
            pltpu.VMEM((full, rank), F32),
            pltpu.VMEM((full, block), BF16),
            pltpu.VMEM((2 * rank, full), BF16),
            pltpu.VMEM((plane, piece, rank), BF16),
            pltpu.VMEM((plane, piece, rank), BF16),
            pltpu.VMEM((modes // 2, piece, rank), F32),
            pltpu.VMEM((piece, rank), F32),
            dma, dma,
            regular((modes // 4 - 1, 2)), regular((2,)), regular, regular((2, 2)),
            dma((modes,)), dma((modes,)),
            dma((plane,)), dma((plane,)),
            dma((modes // 2,)), dma((modes // 2,)),
            dma((plane,)), dma((plane,)),
        ],
        compiler_params=pltpu.CompilerParams(collective_id=0, has_side_effects=True),
        name="exchange",
    )(tensor, start_block)
    return pl.pallas_call(
        finish,
        out_shape=(
            jax.ShapeDtypeStruct((rows, rank), F32),
            jax.ShapeDtypeStruct((block, rank), F32),
        ),
        in_specs=[pl.BlockSpec(memory_space=pltpu.VMEM)] * 2,
        scratch_shapes=[pltpu.VMEM((full, rank), F32)],
        name="finish",
    )(*(pltpu.with_memory_space_constraint(x, pltpu.VMEM) for x in (turned, image)))


def solution(mesh):
    sizes = (mesh.shape["slab"], mesh.shape["mode"])
    return jax.shard_map(
        functools.partial(shards, sizes),
        mesh=mesh,
        in_specs=(P("mode", "slab"), P()),
        out_specs=(P("mode", None), P(("slab", "mode"), None)),
        check_vma=False,
    )
```

```python
import functools

import jax
import jax.numpy as jnp
from jax import lax
from jax.experimental import pallas as pl
from jax.experimental.pallas import tpu as pltpu
from jax.sharding import PartitionSpec as P

MESH = pl.DeviceIdType.MESH
highest = lax.Precision.HIGHEST
BF16, F32 = jnp.bfloat16, jnp.float32


def exchange(sizes, tensor_ref, start_ref, turned_ref, image_ref,
             start, regrouped, split_start, partial_low, plane_in, z_in, mine,
             start_sem, own_sem, z_known, x_known, core_known, y_known, a2a_send, a2a_recv, rs_send, rs_recv,
             z_send, z_recv, ag_send, ag_recv):
    slabs, modes = sizes
    chips_z, plane = modes // 2, slabs * 2
    rows, block = tensor_ref.shape[0], regrouped.shape[1]
    piece = plane_in.shape[1]
    slab, mode = lax.axis_index("slab"), lax.axis_index("mode")
    z, core = mode // 2, lax.rem(mode, 2)
    spot = slab * 2 + core

    def z_peer(dz, flip):
        peer_core = core if flip == 0 else 1 - core
        return lax.rem(z + dz + chips_z, chips_z) * 2 + peer_core

    def plane_peer(offset, sign=1):
        dy, dx, flip = offset
        row = lax.rem(slab // 4 + sign * dy + 4, 4)
        column = lax.rem(lax.rem(slab, 4) + sign * dx + 4, 4)
        return row * 4 + column, core if flip == 0 else 1 - core

    half = chips_z // 2
    order = [half]
    for distance in range(half - 1, 0, -1):
        order += [distance, -distance]
    z_steps = [(dz, flip) for dz in order for flip in (0, 1)] + [(0, 1)]
    side = 4
    x, y = lax.rem(slab, side), slab // side

    def hops(offset):
        return sum(min(d, side - d) for d in offset[:2])

    plane_steps = [(dy, dx, flip) for dy in range(side) for dx in range(side) for flip in (0, 1)][1:]
    plane_steps.sort(key=lambda offset: -hops(offset))
    x_beside = [(y * side + lax.rem(x + d, side), mode) for d in (1, side - 1)]
    y_beside = [(lax.rem(y + d, side) * side + x, mode) for d in (1, side - 1)]
    z_beside = [(slab, z_peer(dz, 0)) for dz in (1, -1)]
    other_core = (slab, z_peer(0, 1))

    def tell(semaphore, device):
        pl.semaphore_signal(semaphore, inc=1, device_id=device, device_id_type=MESH)

    barrier = pltpu.get_barrier_semaphore()
    beside = z_beside + [(slab, z_peer(dz, 1)) for dz in (1, -1)] + [other_core] + x_beside + y_beside
    for device in beside:
        tell(barrier, device)
    own = pltpu.make_async_copy(
        tensor_ref.at[:, pl.ds(pl.multiple_of(mode * block, block), block)],
        regrouped.at[pl.ds(pl.multiple_of(mode * rows, rows), rows), :],
        own_sem,
    )
    own.start()
    fetch = pltpu.make_async_copy(start_ref, start, start_sem)
    fetch.start()
    pl.semaphore_wait(barrier, len(beside))

    def target(dz, flip):
        return z_peer(dz * (1 - 2 * core), flip)

    def source(dz, flip):
        sender = core if flip == 0 else 1 - core
        return z_peer(-dz * (1 - 2 * sender), flip)

    def a2a(index, dz, flip, landing):
        peer = target(dz, flip)
        return pltpu.make_async_remote_copy(
            src_ref=tensor_ref.at[:, pl.ds(pl.multiple_of(peer * block, block), block)],
            dst_ref=regrouped.at[pl.ds(pl.multiple_of(landing * rows, rows), rows), :],
            send_sem=a2a_send.at[index],
            recv_sem=a2a_recv.at[index],
            device_id=(slab, peer),
            device_id_type=MESH,
        )

    def send(distances):
        for index, (dz, flip) in enumerate(z_steps):
            if dz in distances:
                a2a(index, dz, flip, mode).start()

    def reach(known, devices):
        for way in (0, 1):
            tell(known.at[way], devices[way])

    def heard(known):
        for way in (0, 1):
            pl.semaphore_wait(known.at[way], 1)

    reach(z_known.at[0], z_beside)
    reach(x_known, x_beside)
    send((1, -1, 0))
    for further in range(1, half):
        heard(z_known.at[further - 1])
        if further + 1 < half:
            reach(z_known.at[further], z_beside)
        if further == 1:
            send((2, -2))
    send([dz for dz in order if abs(dz) > 2])
    heard(x_known)
    tell(core_known, other_core)
    pl.semaphore_wait(core_known, 1)
    reach(y_known.at[0], y_beside)
    heard(y_known.at[0])
    reach(y_known.at[1], y_beside)
    heard(y_known.at[1])

    fetch.wait()
    start_t = start[...].T
    high = start_t.astype(BF16)
    rank = start.shape[1]
    split_start[:rank, :] = high
    split_start[rank:, :] = (start_t - high.astype(F32)).astype(BF16)

    own.wait()
    for index, (dz, flip) in enumerate(z_steps):
        a2a(index, dz, flip, source(dz, flip)).wait_recv()

    whole = regrouped[...]
    half = whole.shape[1] // 2
    projected = []
    for columns in (whole[:, :half], whole[:, half:]):
        halves = jnp.dot(split_start[...], columns, preferred_element_type=F32)
        projected.append(halves[:rank] + halves[rank:])
    projected = jnp.concatenate(projected, axis=1)
    high = projected.astype(BF16)
    low = (projected - high.astype(F32)).astype(BF16)
    both = jnp.concatenate([high, low], axis=0)
    share = whole.shape[0] // 2
    for part in range(2):
        halves = lax.dot_general(
            whole[part * share : (part + 1) * share], both, (((1,), (1,)), ((), ())), preferred_element_type=F32
        )
        partial = halves[:, :rank] + halves[:, rank:]
        pieces = partial_low.shape[0] // 2
        partial_low[part * pieces : (part + 1) * pieces] = partial.astype(BF16).reshape(
            (pieces,) + partial_low.shape[1:]
        )

    def scatter(index, offset, landing):
        other, peer_core = plane_peer(offset)
        return pltpu.make_async_remote_copy(
            src_ref=partial_low.at[other * 2 + peer_core],
            dst_ref=plane_in.at[landing],
            send_sem=rs_send.at[index],
            recv_sem=rs_recv.at[index],
            device_id=(other, z * 2 + peer_core),
            device_id_type=MESH,
        )

    for index, offset in enumerate(plane_steps):
        scatter(index, offset, spot).start()
    plane_in[spot] = partial_low[spot]
    turned_ref[...] = regrouped[...].T
    for index, (dz, flip) in enumerate(z_steps):
        a2a(index, dz, flip, mode).wait_send()
    for index, offset in reversed(list(enumerate(plane_steps))):
        other, peer_core = plane_peer(offset, -1)
        scatter(index, offset, other * 2 + peer_core).wait_recv()
    mine[...] = jnp.sum(plane_in[...].astype(F32), axis=0)
    z_in[z] = mine[...]

    def along_z(index, dz, landing):
        peer = target(dz, 0)
        return pltpu.make_async_remote_copy(
            src_ref=mine,
            dst_ref=z_in.at[landing],
            send_sem=z_send.at[index],
            recv_sem=z_recv.at[index],
            device_id=(slab, peer),
            device_id_type=MESH,
        )

    for index, dz in enumerate(order):
        along_z(index, dz, z).start()
    for index, offset in enumerate(plane_steps):
        scatter(index, offset, spot).wait_send()
    for index, dz in reversed(list(enumerate(order))):
        along_z(index, dz, source(dz, 0) // 2).wait_recv()
    image_ref[spot] = jnp.sum(z_in[...], axis=0)

    def gather(index, offset, landing):
        other, peer_core = plane_peer(offset)
        return pltpu.make_async_remote_copy(
            src_ref=image_ref.at[spot],
            dst_ref=image_ref.at[landing],
            send_sem=ag_send.at[index],
            recv_sem=ag_recv.at[index],
            device_id=(other, z * 2 + peer_core),
            device_id_type=MESH,
        )

    for index, offset in enumerate(plane_steps):
        gather(index, offset, spot).start()
    for index, dz in enumerate(order):
        along_z(index, dz, z).wait_send()
    for index, offset in enumerate(plane_steps):
        gather(index, offset, spot).wait_send()
    for index, offset in reversed(list(enumerate(plane_steps))):
        other, peer_core = plane_peer(offset, -1)
        gather(index, offset, other * 2 + peer_core).wait_recv()


def inverse_factor(gram):
    n = gram.shape[0]
    tall = n // 8
    lane = lax.broadcasted_iota(jnp.int32, (8, n), 1)
    sub = lax.broadcasted_iota(jnp.int32, (8, n), 0)
    spread = lambda x, k: jnp.broadcast_to(x[:, k : k + 1], (8, n))
    pick = lambda x, k: jnp.broadcast_to(x[k : k + 1], (8, n))
    work = [gram[8 * r : 8 * r + 8, :] for r in range(tall)]
    nothing = work[0] * 0.0
    ahead = [spread(work[0], k) + nothing for k in range(8)]
    out = []
    for p in range(tall):
        cols, more = ahead, p + 1 < tall
        far = {r: [spread(work[r], 8 * p + k) for k in range(8)] for r in range(p + 1, tall)}
        if more:
            beside = [x + nothing for x in far[p + 1]]
            ahead = [spread(work[p + 1], 8 * (p + 1) + k) for k in range(8)]
        rows = work[p]
        done = nothing
        for s in range(0, 8, 2):
            j = 8 * p + s
            col_a, col_b = cols[s], cols[s + 1]
            a, b, c = pick(col_a, s), pick(col_a, s + 1), pick(col_b, s + 1)
            det = a * c - b * b
            inv = 1.0 / det
            ia, ib, ic = c * inv, b * inv, a * inv
            mul_a, mul_b = ia * col_a - ib * col_b, ic * col_b - ib * col_a
            if more:
                next_a, next_b = beside[s], beside[s + 1]
                low_a, low_b = ia * next_a - ib * next_b, ic * next_b - ib * next_a
                for k in range(8):
                    ahead[k] = ahead[k] - (low_a * pick(next_a, k) + low_b * pick(next_b, k))
                for k in range(s + 2, 8):
                    beside[k] = beside[k] - (low_a * pick(cols[k], s) + low_b * pick(cols[k], s + 1))
            row_a, row_b = pick(rows, s), pick(rows, s + 1)
            unit_a = jnp.where(lane == j, 1.0, 0.0).astype(F32)
            unit_b = jnp.where(lane == j + 1, 1.0, 0.0).astype(F32)
            left_a = jnp.where(lane < j, row_a, unit_a)
            left_b = jnp.where(lane < j, row_b, unit_b)
            root_a = lax.rsqrt(a)
            root_b = lax.rsqrt(det * (root_a * root_a))
            w_a = left_a * root_a
            w_b = (left_b - (b * root_a) * w_a) * root_b
            done = jnp.where(sub == s, w_a, jnp.where(sub == s + 1, w_b, done))
            if s < 6:
                rows = jnp.where((lane == j) | (lane == j + 1), 0.0, rows) - (mul_a * left_a + mul_b * left_b)
            swept_a = jnp.where(sub == s, 1.0 - ia, jnp.where(sub == s + 1, ib, mul_a))
            swept_b = jnp.where(sub == s, ib, jnp.where(sub == s + 1, 1.0 - ic, mul_b))
            for k in range(8):
                if k < s or (k > s + 1):
                    if more or k > s + 1:
                        cols[k] = cols[k] - (swept_a * pick(cols[k], s) + swept_b * pick(cols[k], s + 1))
            cols[s] = jnp.where(sub == s, 1.0, 0.0) - swept_a
            cols[s + 1] = jnp.where(sub == s + 1, 1.0, 0.0) - swept_b
        out.append(done)
        if more:
            within = (lane >= 8 * p) & (lane < 8 * p + 8)
            terms = [
                cols[k] * jnp.where(within, jnp.where(lane == 8 * p + k, 1.0, 0.0), pick(work[p], k))
                for k in range(8)
            ]
            solved = ((terms[0] + terms[1]) + (terms[2] + terms[3])) + ((terms[4] + terms[5]) + (terms[6] + terms[7]))
            against = [pick(solved, k) for k in range(8)]
            for r in range(p + 1, tall):
                terms = [far[r][k] * against[k] for k in range(8)]
                total = ((terms[0] + terms[1]) + (terms[2] + terms[3])) + ((terms[4] + terms[5]) + (terms[6] + terms[7]))
                work[r] = jnp.where(within, 0.0, work[r]) - total
    return jnp.concatenate(out, axis=0)


def finish(turned_ref, image_ref, rows_ref, core_ref, basis):
    image = image_ref[...].reshape(basis.shape)
    image = image * lax.rsqrt(jnp.sum(image * image, axis=0, keepdims=True))
    across = (((0,), (0,)), ((), ()))
    half = image.shape[0] // 2
    gram = sum(
        lax.dot_general(rows, rows, across, precision=highest, preferred_element_type=F32)
        for rows in (image[:half], image[half:])
    )
    inverse = inverse_factor(gram)
    turned_inverse = inverse.T
    inverse_high = turned_inverse.astype(BF16)
    inverse_low = (turned_inverse - inverse_high.astype(F32)).astype(BF16)
    both = jnp.concatenate([inverse_high, inverse_low], axis=1)
    rank = image.shape[1]
    image_high = image.astype(BF16)
    image_low = (image - image_high.astype(F32)).astype(BF16)
    whole = []
    for part in (slice(0, half), slice(half, None)):
        halves = jnp.dot(image_high[part], both, preferred_element_type=F32)
        lower = jnp.dot(image_low[part], inverse_high, preferred_element_type=F32)
        whole.append(halves[:, :rank] + (halves[:, rank:] + lower))
    whole = jnp.concatenate(whole, axis=0)
    basis[...] = whole
    count = rows_ref.shape[0]
    rows_ref[...] = basis[pl.ds(pl.multiple_of(lax.axis_index("mode") * count, count), count), :]
    core_ref[...] = jnp.dot(turned_ref[...], whole.astype(BF16), preferred_element_type=F32)


def shards(sizes, tensor, start_block):
    slabs, modes = sizes
    rows, width = tensor.shape
    full, rank = start_block.shape
    block = width // modes
    plane = slabs * 2
    piece = full // plane
    dma, regular = pltpu.SemaphoreType.DMA, pltpu.SemaphoreType.REGULAR
    turned, image = pl.pallas_call(
        functools.partial(exchange, sizes),
        out_shape=(
            pltpu.VMEM((block, full), BF16),
            pltpu.VMEM((plane, piece, rank), F32),
        ),
        in_specs=[pl.BlockSpec(memory_space=pl.ANY)] * 2,
        out_specs=(pl.BlockSpec(memory_space=pltpu.VMEM), pl.BlockSpec(memory_space=pltpu.VMEM)),
        scratch_shapes=[
            pltpu.VMEM((full, rank), F32),
            pltpu.VMEM((full, block), BF16),
            pltpu.VMEM((2 * rank, full), BF16),
            pltpu.VMEM((plane, piece, rank), BF16),
            pltpu.VMEM((plane, piece, rank), BF16),
            pltpu.VMEM((modes // 2, piece, rank), F32),
            pltpu.VMEM((piece, rank), F32),
            dma, dma,
            regular((modes // 4 - 1, 2)), regular((2,)), regular, regular((2, 2)),
            dma((modes,)), dma((modes,)),
            dma((plane,)), dma((plane,)),
            dma((modes // 2,)), dma((modes // 2,)),
            dma((plane,)), dma((plane,)),
        ],
        compiler_params=pltpu.CompilerParams(collective_id=0, has_side_effects=True),
        name="exchange",
    )(tensor, start_block)
    return pl.pallas_call(
        finish,
        out_shape=(
            jax.ShapeDtypeStruct((rows, rank), F32),
            jax.ShapeDtypeStruct((block, rank), F32),
        ),
        in_specs=[pl.BlockSpec(memory_space=pltpu.VMEM)] * 2,
        scratch_shapes=[pltpu.VMEM((full, rank), F32)],
        name="finish",
    )(*(pltpu.with_memory_space_constraint(x, pltpu.VMEM) for x in (turned, image)))


def solution(mesh):
    sizes = (mesh.shape["slab"], mesh.shape["mode"])
    return jax.shard_map(
        functools.partial(shards, sizes),
        mesh=mesh,
        in_specs=(P("mode", "slab"), P()),
        out_specs=(P("mode", None), P(("slab", "mode"), None)),
        check_vma=False,
    )
```
